768 devices in a mesh: gx: 32 (over y, x_lo, core), gy: 24 (over x_hi, z).
Axes of the slice: x: 4 (x_hi: 2, x_lo: 2; x = x_hi * 2 + x_lo), y: 8, z: 12, core: 2. Of those that a mesh axis runs over, the one named last changes fastest.
Arguments:
- u_flow: bfloat16 [16, 4608, 3072], P(None, 'gx', 'gy'), may hold values from -6 to 6
- v_flow: bfloat16 [16, 4608, 3072], P(None, 'gx', 'gy'), may hold values from -6 to 6
- sea_mask: int32 [4608, 3072], P('gx', 'gy'), may hold values 0 or 1
- bottom_level: int32 [4608, 3072], P('gx', 'gy'), may hold values from 1 to 16
- mode_project: bfloat16 [16, 2], replicated, may hold values from -1.5 to 1.5
- mode_shape: float32 [16, 2], replicated, may hold values from -4 to 4
- forward_x: bfloat16 [4608, 4608], P('gx'), may hold values from -0.09375 to 0.09375
- forward_y: bfloat16 [3072, 3072], P('gy'), may hold values from -0.109375 to 0.109375
- inverse_x: bfloat16 [4608, 4608], P('gx'), may hold values from -0.09375 to 0.09375
- inverse_y: bfloat16 [3072, 3072], P('gy'), may hold values from -0.109375 to 0.109375
- eigen_x: float32 [4608], P('gx'), may hold values from 0.5 to 4
- eigen_y: float32 [3072], P('gy'), may hold values from 0.5 to 4
- mode_shift: float32 [2], replicated, may hold values from 0.5 to 2
Outputs:
- u_correct: bfloat16 [16, 4608, 3072], P(None, 'gx', 'gy')
- v_correct: bfloat16 [16, 4608, 3072], P(None, 'gx', 'gy')
- pressure: float32 [2, 4608, 3072], P(None, 'gx', 'gy')
The draws below stay inside these ranges and needn't reach their ends.
Inputs may be any that keep to these rules, and one draw needn't show every extreme that they name: `sea_mask`: land and sea flags.
All inputs are finite; a program needn't handle non-finite values. No bound on the sum of `sea_mask` on one device may be relied on, other than what follows from the above.
Results may differ from the reference program's by a relative error of at most 0.014.
Values may be sent and summed in bfloat16 or wider, within the bound.
No kernel may reach another device: no remote copies, remote signals or barrier semaphores. Data moves between devices by JAX's collectives and lax.ppermute only.
A program may use at most 32 MiB of HBM per device.

```python
import math
import jax
import jax.numpy as jnp
from jax import lax

LEV = 16
MODES = 2
NX = 4608
NY = 3072


def with_ends(result, key, least, top_value):
    longest = result.shape.index(max(result.shape))
    spots = []
    for shift in (0, 1):
        where = [jax.random.randint(jax.random.fold_in(key, axis), (), 0, length) for axis, length in enumerate(result.shape)]
        where[longest] = (where[longest] + shift) % result.shape[longest]
        spots.append(tuple(where))
    return result.at[spots[0]].set(least).at[spots[1]].set(top_value)


def steps_of(key, dims, shards, low, high):
    loudness, own = 1.0, jax.random.fold_in(key, 6)
    for axis_at, blocks in shards:
        heights = jnp.exp(jax.random.uniform(jax.random.fold_in(own, axis_at), (blocks,), jnp.float32, low / len(shards), high / len(shards)))
        loudness = loudness * jnp.repeat(heights, dims[axis_at] // blocks).reshape([-1 if axis == axis_at else 1 for axis in range(len(dims))])
    return loudness


def bell_draw(rng, dims, deviation, limit, shards=(), kind=jnp.bfloat16):
    drawn = jax.random.normal(rng, dims, jnp.float32) * deviation
    if len(shards) > 0:
        drawn = steps_of(rng, dims, shards, -0.22, 0.18) * drawn
    return jnp.clip(drawn, min=-limit, max=limit).astype(kind)


def setup_inputs(seed: int = 0) -> dict:
    keys = jax.random.split(jax.random.key(seed), 14)
    u_flow = bell_draw(keys[0], (LEV, NX, NY), 1.0, 6.0, ((1, 32), (2, 24)))
    v_flow = bell_draw(keys[1], (LEV, NX, NY), 1.0, 6.0, ((1, 32), (2, 24)))
    sea_mask = with_ends((jax.random.randint(keys[2], (NX, NY), 0, 4) < 3).astype(jnp.int32), jax.random.fold_in(keys[2], 1), 0, 1)
    bottom_level = with_ends(jax.random.randint(keys[3], (NX, NY), 1, LEV + 1), jax.random.fold_in(keys[3], 1), 1, LEV).astype(jnp.int32)
    mode_project = bell_draw(keys[4], (LEV, MODES), LEV ** -0.5, 1.5)
    mode_shape = bell_draw(keys[5], (LEV, MODES), 1.0, 4.0, (), jnp.float32)
    forward_x = bell_draw(keys[6], (NX, NX), NX ** -0.5, 0.09375, ((0, 32),))
    forward_y = bell_draw(keys[7], (NY, NY), NY ** -0.5, 0.109375, ((0, 24),))
    inverse_x = bell_draw(keys[8], (NX, NX), NX ** -0.5, 0.09375, ((0, 32),))
    inverse_y = bell_draw(keys[9], (NY, NY), NY ** -0.5, 0.109375, ((0, 24),))
    eigen_x = jnp.clip(jnp.exp(math.log(4.0) - 2.0794415 * jax.random.uniform(keys[10], (NX,), jnp.float32) ** steps_of(keys[10], (NX,), ((0, 32),), -0.2, 0.2)), 0.5, 4.0)
    eigen_y = jnp.clip(jnp.exp(math.log(4.0) - 2.0794415 * jax.random.uniform(keys[11], (NY,), jnp.float32) ** steps_of(keys[11], (NY,), ((0, 24),), -0.2, 0.2)), 0.5, 4.0)
    mode_shift = jnp.clip(jnp.exp(jax.random.uniform(keys[12], (MODES,), jnp.float32, math.log(0.5), math.log(2.0))), 0.5, 2.0)
    return dict(u_flow=u_flow, v_flow=v_flow, sea_mask=sea_mask, bottom_level=bottom_level, mode_project=mode_project, mode_shape=mode_shape, forward_x=forward_x, forward_y=forward_y, inverse_x=inverse_x, inverse_y=inverse_y, eigen_x=eigen_x, eigen_y=eigen_y, mode_shift=mode_shift)


def shifted_y(field, step):
    padded = jnp.pad(field, ((0, 0), (0, 0), (1, 1)))
    if step > 0:
        return padded[:, :, 2:]
    return padded[:, :, :-2]


def reference(u_flow, v_flow, sea_mask, bottom_level, mode_project, mode_shape, forward_x, forward_y, inverse_x, inverse_y, eigen_x, eigen_y, mode_shift):
    high = lax.Precision.HIGHEST
    mask_f = sea_mask.astype(jnp.float32)
    level_ids = jnp.arange(LEV, dtype=jnp.int32)

    def project(carry, inputs):
        acc_u, acc_v = carry
        u_level, v_level, weights, level = inputs
        wet = mask_f * (level < bottom_level).astype(jnp.float32)
        w32 = weights.astype(jnp.float32)[:, None, None]
        acc_u = acc_u + w32 * (wet * u_level.astype(jnp.float32))[None]
        acc_v = acc_v + w32 * (wet * v_level.astype(jnp.float32))[None]
        return (acc_u, acc_v), None

    zeros = jnp.zeros((MODES, NX, NY), jnp.float32)
    (flux_u, flux_v), _ = lax.scan(project, (zeros, zeros), (u_flow, v_flow, mode_project, level_ids))
    flux_u = flux_u.astype(jnp.bfloat16).astype(jnp.float32)
    flux_v = flux_v.astype(jnp.bfloat16).astype(jnp.float32)
    divergence = mask_f[None] * (0.5 * (jnp.roll(flux_u, -1, 1) - jnp.roll(flux_u, 1, 1)) + 0.5 * (shifted_y(flux_v, 1) - shifted_y(flux_v, -1)))
    divergence = divergence.astype(jnp.bfloat16)
    spec_x = jnp.einsum('ki,mij->mkj', forward_x.astype(jnp.float32), divergence.astype(jnp.float32), precision=high).astype(jnp.bfloat16)
    spec_xy = jnp.einsum('qj,mkj->mkq', forward_y.astype(jnp.float32), spec_x.astype(jnp.float32), precision=high)
    denom = eigen_x[None, :, None] + eigen_y[None, None, :] + mode_shift[:, None, None]
    scaled = (spec_xy / denom).astype(jnp.bfloat16)
    back_y = jnp.einsum('jq,mkq->mkj', inverse_y.astype(jnp.float32), scaled.astype(jnp.float32), precision=high).astype(jnp.bfloat16)
    pressure = jnp.einsum('ik,mkj->mij', inverse_x.astype(jnp.float32), back_y.astype(jnp.float32), precision=high)
    grad_x = 0.5 * (jnp.roll(pressure, -1, 1) - jnp.roll(pressure, 1, 1))
    grad_y = 0.5 * (shifted_y(pressure, 1) - shifted_y(pressure, -1))

    def rebuild(inputs):
        shape_row, level = inputs
        wet = mask_f * (level < bottom_level).astype(jnp.float32)
        corr_u = -wet * (shape_row[0] * grad_x[0] + shape_row[1] * grad_x[1])
        corr_v = -wet * (shape_row[0] * grad_y[0] + shape_row[1] * grad_y[1])
        return corr_u.astype(jnp.bfloat16), corr_v.astype(jnp.bfloat16)

    u_correct, v_correct = lax.map(rebuild, (mode_shape, level_ids))
    return u_correct, v_correct, pressure
```

```python
import jax
import jax.numpy as jnp
from jax import lax
from jax.sharding import Mesh
from jax.sharding import PartitionSpec as P

SUB = (("y", 8), ("xl", 2), ("c", 2), ("xh", 2), ("zh", 3), ("zl", 4))
GX = ("y", "xl", "c")
GY = ("xh", "zh", "zl")
QUAD = ("xl", "c")
BF = jnp.bfloat16
F32 = jnp.float32


def gather(block, axes, count):
    return lax.all_to_all(jnp.broadcast_to(block[None], (count,) + block.shape), axes, 0, 0)


def scatter_sum(parts, axes):
    return jnp.sum(lax.all_to_all(parts, axes, 0, 0).astype(F32), axis=0)


def edges(block, axes, dim, count, periodic):
    forward = [(i, i + 1) for i in range(count - 1)]
    if periodic:
        forward.append((count - 1, 0))
    backward = [(target, source) for source, target in forward]
    low = lax.ppermute(lax.slice_in_dim(block, block.shape[dim] - 1, None, axis=dim), axes, forward)
    high = lax.ppermute(lax.slice_in_dim(block, 0, 1, axis=dim), axes, backward)
    return low, high


def centre_x(field):
    low, high = edges(field.astype(BF), GX, 1, 32, True)
    padded = jnp.concatenate([low.astype(F32), field, high.astype(F32)], axis=1)
    return 0.5 * (padded[:, 2:, :] - padded[:, :-2, :])


def centre_y(field):
    low, high = edges(field.astype(BF), GY, 2, 24, False)
    padded = jnp.concatenate([low.astype(F32), field, high.astype(F32)], axis=2)
    return 0.5 * (padded[:, :, 2:] - padded[:, :, :-2])


def quad_tables(fx, ix):
    me = lax.axis_index("xl") * 2 + lax.axis_index("c")
    both = jnp.stack([fx, ix]).reshape(2, 144, 8, 4, 144)
    both = jnp.moveaxis(both, 3, 0).reshape(4, 2, 144, 1152)
    pieces = [lax.dynamic_index_in_dim(both, me, 0, False)]
    for step in (1, 2, 3):
        send = lax.dynamic_index_in_dim(both, me ^ step, 0, False)
        pieces.append(lax.ppermute(send, QUAD, [(i, i ^ step) for i in range(4)]))
    held = jnp.stack(pieces)
    ordered = jnp.stack([lax.dynamic_index_in_dim(held, me ^ i, 0, False) for i in range(4)])
    return ordered[:, 0].reshape(576, 1152), ordered[:, 1].reshape(576, 1152)


def ring_tables(fy, iy):
    me = lax.axis_index("zh")
    both = jnp.stack([fy, iy]).reshape(2, 128, 2, 3, 512)
    both = jnp.moveaxis(both, 3, 0).reshape(3, 2, 128, 1024)
    pieces = [lax.dynamic_index_in_dim(both, me, 0, False)]
    for step in (1, 2):
        send = lax.dynamic_index_in_dim(both, (me + step) % 3, 0, False)
        pieces.append(lax.ppermute(send, "zh", [(i, (i + step) % 3) for i in range(3)]))
    held = jnp.stack(pieces)
    ordered = jnp.stack([lax.dynamic_index_in_dim(held, (me + 3 - i) % 3, 0, False) for i in range(3)])
    return ordered[:, 0], ordered[:, 1]


def transform_x(block, table):
    held = gather(block, "y", 8).reshape(1152, 256)
    parts = jnp.dot(table, held, preferred_element_type=F32).astype(BF)
    return scatter_sum(parts.reshape(4, 144, 256), QUAD)


def transform_y(block, table):
    held = gather(block, ("xh", "zl"), 8)
    parts = jnp.einsum("bkj,tqbj->tkq", held, table.reshape(3, 128, 8, 128), preferred_element_type=F32)
    return scatter_sum(parts.astype(BF), "zh")


def to_x(block):
    return jnp.concatenate([block[:144], block[144:]], axis=1)


def to_y(block):
    return jnp.concatenate([block[:, :128], block[:, 128:]], axis=0)


def body(
    u_flow,
    v_flow,
    sea_mask,
    bottom_level,
    mode_project,
    mode_shape,
    forward_x,
    forward_y,
    inverse_x,
    inverse_y,
    eigen_x,
    eigen_y,
    mode_shift,
):
    level_ids = lax.broadcasted_iota(jnp.int32, u_flow.shape, 0)
    wet_int = sea_mask[None] * (level_ids < bottom_level[None]).astype(jnp.int32)
    wet = wet_int.astype(BF)
    flux_u = jnp.einsum("lm,lij->mij", mode_project, u_flow * wet, preferred_element_type=F32)
    flux_v = jnp.einsum("lm,lij->mij", mode_project, v_flow * wet, preferred_element_type=F32)
    flux_u = flux_u.astype(BF).astype(F32)
    flux_v = flux_v.astype(BF).astype(F32)
    mask_f = sea_mask.astype(F32)
    divergence = (mask_f[None] * (centre_x(flux_u) + centre_y(flux_v))).astype(BF)
    table_fx, table_ix = quad_tables(forward_x, inverse_x)
    table_fy, table_iy = ring_tables(forward_y, inverse_y)
    spec_x = transform_x(to_x(divergence.reshape(288, 128)), table_fx).astype(BF)
    spec_xy = transform_y(to_y(spec_x), table_fy).reshape(2, 144, 128)
    denom = eigen_x[None, :, None] + eigen_y[None, None, :] + mode_shift[:, None, None]
    scaled = (spec_xy / denom).astype(BF)
    back_y = transform_y(scaled.reshape(288, 128), table_iy).astype(BF)
    pressure = to_y(transform_x(to_x(back_y), table_ix)).reshape(2, 144, 128)
    grad_x = centre_x(pressure)
    grad_y = centre_y(pressure)
    wet_f = wet_int.astype(F32)
    shape_zero = mode_shape[:, 0][:, None, None]
    shape_one = mode_shape[:, 1][:, None, None]
    u_correct = (-wet_f * (shape_zero * grad_x[0][None] + shape_one * grad_x[1][None])).astype(BF)
    v_correct = (-wet_f * (shape_zero * grad_y[0][None] + shape_one * grad_y[1][None])).astype(BF)
    return (u_correct, v_correct, pressure)


def solution(mesh):
    sub = Mesh(mesh.devices.reshape([n for _, n in SUB]), [name for name, _ in SUB])
    return jax.shard_map(
        body,
        mesh=sub,
        in_specs=(
            P(None, GX, GY),
            P(None, GX, GY),
            P(GX, GY),
            P(GX, GY),
            P(),
            P(),
            P(GX, None),
            P(GY, None),
            P(GX, None),
            P(GY, None),
            P(GX),
            P(GY),
            P(),
        ),
        out_specs=(P(None, GX, GY), P(None, GX, GY), P(None, GX, GY)),
        check_vma=False,
    )
```

```python
import functools

import jax
import jax.numpy as jnp
from jax import lax
from jax.experimental import pallas as pl
from jax.experimental.pallas import tpu as pltpu
from jax.sharding import Mesh
from jax.sharding import PartitionSpec as P

SUB = (("y", 8), ("xl", 2), ("c", 2), ("xh", 2), ("zh", 4), ("zl", 3))
GX = ("y", "xl", "c")
GY = ("xh", "zh", "zl")
QUAD = ("xl", "c")
BF = jnp.bfloat16
F32 = jnp.float32


def gather(block, axes, count):
    return lax.all_to_all(jnp.broadcast_to(block[None], (count,) + block.shape), axes, 0, 0)


def scatter_sum(parts, axes):
    return jnp.sum(lax.all_to_all(parts, axes, 0, 0).astype(F32), axis=0)


def edges(block, axes, dim, count, periodic):
    forward = [(i, i + 1) for i in range(count - 1)]
    if periodic:
        forward.append((count - 1, 0))
    backward = [(target, source) for source, target in forward]
    low = lax.ppermute(lax.slice_in_dim(block, block.shape[dim] - 1, None, axis=dim), axes, forward)
    high = lax.ppermute(lax.slice_in_dim(block, 0, 1, axis=dim), axes, backward)
    return low, high


def centre_x(field):
    low, high = edges(field.astype(BF), GX, 1, 32, True)
    padded = jnp.concatenate([low.astype(F32), field, high.astype(F32)], axis=1)
    return 0.5 * (padded[:, 2:, :] - padded[:, :-2, :])


def centre_y(field):
    low, high = edges(field.astype(BF), GY, 2, 24, False)
    padded = jnp.concatenate([low.astype(F32), field, high.astype(F32)], axis=2)
    return 0.5 * (padded[:, :, 2:] - padded[:, :, :-2])


def call(kernel, out_shape, operands, scratch=(), flops=0):
    smem, vmem = pl.BlockSpec(memory_space=pltpu.SMEM), pl.BlockSpec(memory_space=pltpu.VMEM)
    outs = out_shape if isinstance(out_shape, list) else [out_shape]
    moved = sum(x.size * x.dtype.itemsize for x in list(operands[1:]) + outs)
    return pl.pallas_call(
        kernel,
        out_shape=out_shape,
        in_specs=[smem] + [vmem] * (len(operands) - 1),
        out_specs=[vmem] * len(outs) if isinstance(out_shape, list) else vmem,
        scratch_shapes=list(scratch),
        cost_estimate=pl.CostEstimate(flops=flops, bytes_accessed=moved, transcendentals=0),
        compiler_params=pltpu.CompilerParams(vmem_limit_bytes=24 << 20),
    )(*operands)


def window(place, half):
    return 9 * (place // 2) + 4 * (place % 2) + half


def quad_cut_kernel(me_ref, rows_ref, *out_refs):
    me = me_ref[0]
    for step, out_ref in enumerate(out_refs):
        other = lax.bitwise_xor(me, step)
        for y in range(8):
            start = pl.multiple_of((window(y, 0) + other) * 128, 128)
            out_ref[:, y * 256 : (y + 1) * 256] = rows_ref[:, pl.ds(start, 256)]


def quad_cut(me, rows):
    return call(quad_cut_kernel, [jax.ShapeDtypeStruct((144, 2048), BF)] * 4, (me, rows))


def quad_send(piece, step):
    return lax.ppermute(piece, QUAD, [(i, i ^ step) for i in range(4)])


def ring_cut_kernel(me_ref, first_ref, second_ref, *out_refs):
    me = me_ref[0]
    for step, out_ref in enumerate(out_refs):
        other = lax.rem(me + step, 3)
        for g in range(8):
            start = pl.multiple_of((3 * g + other) * 128, 128)
            out_ref[:128, g * 128 : (g + 1) * 128] = first_ref[:, pl.ds(start, 128)]
            out_ref[128:, g * 128 : (g + 1) * 128] = second_ref[:, pl.ds(start, 128)]


def ring_tables(me, first, second):
    pieces = call(ring_cut_kernel, [jax.ShapeDtypeStruct((256, 1024), BF)] * 3, (me, first, second))
    moved = [
        lax.ppermute(pieces[step], "zl", [(i, (i + step) % 3) for i in range(3)]) for step in (1, 2)
    ]
    return [pieces[0]] + moved


def x_kernel(me_ref, held_ref, t0, t1, t2, t3, out_ref, placed):
    me = me_ref[0]
    placed[...] = jnp.zeros_like(placed)
    for y in range(8):
        start = pl.multiple_of(256 * y + 64 * (y % 2) + 16 * me, 16)
        placed[pl.ds(start, 144), :] = held_ref[y]
    for step, table in enumerate((t0, t1, t2, t3)):
        part = jnp.dot(table[...], placed[...], preferred_element_type=F32)
        out_ref[lax.bitwise_xor(me, step)] = part.astype(BF)


def transform_x(me, block, table):
    held = gather(block, "y", 8)
    parts = call(
        x_kernel,
        jax.ShapeDtypeStruct((4, 144, 256), BF),
        (me, held, *table),
        [pltpu.VMEM((2048, 256), BF)],
        flops=2 * 576 * 2048 * 256,
    )
    return scatter_sum(parts, QUAD)


def y_kernel(offset, me_ref, held_ref, t0, t1, t2, out_ref, placed):
    me = me_ref[0]
    for g in range(8):
        placed[:, g * 128 : (g + 1) * 128] = held_ref[g]
    for step, table in enumerate((t0, t1, t2)):
        part = lax.dot_general(
            placed[...],
            table[offset : offset + 128, :],
            (((1,), (1,)), ((), ())),
            preferred_element_type=F32,
        )
        out_ref[lax.rem(me + 3 - step, 3)] = part.astype(BF)


def transform_y(me, block, table, offset):
    held = gather(block, ("xh", "zh"), 8)
    parts = call(
        functools.partial(y_kernel, offset),
        jax.ShapeDtypeStruct((3, 288, 128), BF),
        (me, held, *table),
        [pltpu.VMEM((288, 1024), BF)],
        flops=2 * 288 * 1024 * 384,
    )
    return scatter_sum(parts, "zl")


def to_x(block):
    return jnp.concatenate([block[:144], block[144:]], axis=1)


def to_y(block):
    return jnp.concatenate([block[:, :128], block[:, 128:]], axis=0)


def body(
    u_flow,
    v_flow,
    sea_mask,
    bottom_level,
    mode_project,
    mode_shape,
    forward_x,
    forward_y,
    inverse_x,
    inverse_y,
    eigen_x,
    eigen_y,
    mode_shift,
):
    level_ids = lax.broadcasted_iota(jnp.int32, u_flow.shape, 0)
    wet_int = sea_mask[None] * (level_ids < bottom_level[None]).astype(jnp.int32)
    wet = wet_int.astype(BF)
    flux_u = jnp.einsum("lm,lij->mij", mode_project, u_flow * wet, preferred_element_type=F32)
    flux_v = jnp.einsum("lm,lij->mij", mode_project, v_flow * wet, preferred_element_type=F32)
    flux_u = flux_u.astype(BF).astype(F32)
    flux_v = flux_v.astype(BF).astype(F32)
    mask_f = sea_mask.astype(F32)
    divergence = (mask_f[None] * (centre_x(flux_u) + centre_y(flux_v))).astype(BF)
    quad_me = (lax.axis_index("xl") * 2 + lax.axis_index("c")).astype(jnp.int32).reshape(1)
    ring_me = lax.axis_index("zl").astype(jnp.int32).reshape(1)
    cut_fx = quad_cut(quad_me, forward_x)
    divergence, fx_two = lax.optimization_barrier((divergence, quad_send(cut_fx[2], 2)))
    table_fx = (cut_fx[0], quad_send(cut_fx[1], 1), fx_two, quad_send(cut_fx[3], 3))
    table_y = ring_tables(ring_me, forward_y, inverse_y)
    spec_x = transform_x(quad_me, to_x(divergence.reshape(288, 128)), table_fx).astype(BF)
    spec_x, table_y = lax.optimization_barrier((spec_x, table_y))
    spec_xy = transform_y(ring_me, to_y(spec_x), table_y, 0).reshape(2, 144, 128)
    denom = eigen_x[None, :, None] + eigen_y[None, None, :] + mode_shift[:, None, None]
    scaled = (spec_xy / denom).astype(BF)
    back_y = transform_y(ring_me, scaled.reshape(288, 128), table_y, 128).astype(BF)
    cut_ix = quad_cut(quad_me, inverse_x)
    back_y, ix_two = lax.optimization_barrier((back_y, quad_send(cut_ix[2], 2)))
    table_ix = (cut_ix[0], quad_send(cut_ix[1], 1), ix_two, quad_send(cut_ix[3], 3))
    pressure = to_y(transform_x(quad_me, to_x(back_y), table_ix)).reshape(2, 144, 128)
    grad_x = centre_x(pressure)
    grad_y = centre_y(pressure)
    wet_f = wet_int.astype(F32)
    shape_zero = mode_shape[:, 0][:, None, None]
    shape_one = mode_shape[:, 1][:, None, None]
    u_correct = (-wet_f * (shape_zero * grad_x[0][None] + shape_one * grad_x[1][None])).astype(BF)
    v_correct = (-wet_f * (shape_zero * grad_y[0][None] + shape_one * grad_y[1][None])).astype(BF)
    return (u_correct, v_correct, pressure)


def solution(mesh):
    sub = Mesh(mesh.devices.reshape([n for _, n in SUB]), [name for name, _ in SUB])
    return jax.shard_map(
        body,
        mesh=sub,
        in_specs=(
            P(None, GX, GY),
            P(None, GX, GY),
            P(GX, GY),
            P(GX, GY),
            P(),
            P(),
            P(GX, None),
            P(GY, None),
            P(GX, None),
            P(GY, None),
            P(GX),
            P(GY),
            P(),
        ),
        out_specs=(P(None, GX, GY), P(None, GX, GY), P(None, GX, GY)),
        check_vma=False,
    )
```

```python
import functools

import jax
import jax.numpy as jnp
from jax import lax
from jax.experimental import pallas as pl
from jax.experimental.pallas import tpu as pltpu
from jax.sharding import Mesh
from jax.sharding import PartitionSpec as P

SUB = (("y", 8), ("xl", 2), ("c", 2), ("xh", 2), ("zh", 4), ("zl", 3))
GX = ("y", "xl", "c")
GY = ("xh", "zh", "zl")
QUAD = ("xl", "c")
BF = jnp.bfloat16
F32 = jnp.float32


def gather(block, axes, count):
    return lax.all_to_all(jnp.broadcast_to(block[None], (count,) + block.shape), axes, 0, 0)


def scatter_sum(parts, axes):
    return jnp.sum(lax.all_to_all(parts, axes, 0, 0).astype(F32), axis=0)


def edges(block, axes, dim, count, periodic):
    forward = [(i, i + 1) for i in range(count - 1)]
    if periodic:
        forward.append((count - 1, 0))
    backward = [(target, source) for source, target in forward]
    low = lax.ppermute(lax.slice_in_dim(block, block.shape[dim] - 1, None, axis=dim), axes, forward)
    high = lax.ppermute(lax.slice_in_dim(block, 0, 1, axis=dim), axes, backward)
    return low, high


def centre_x(field):
    low, high = edges(field.astype(BF), GX, 1, 32, True)
    padded = jnp.concatenate([low.astype(F32), field, high.astype(F32)], axis=1)
    return 0.5 * (padded[:, 2:, :] - padded[:, :-2, :])


def centre_y(field):
    low, high = edges(field.astype(BF), GY, 2, 24, False)
    padded = jnp.concatenate([low.astype(F32), field, high.astype(F32)], axis=2)
    return 0.5 * (padded[:, :, 2:] - padded[:, :, :-2])


def call(kernel, out_shape, operands, scratch=(), flops=0):
    smem, vmem = pl.BlockSpec(memory_space=pltpu.SMEM), pl.BlockSpec(memory_space=pltpu.VMEM)
    outs = out_shape if isinstance(out_shape, list) else [out_shape]
    moved = sum(x.size * x.dtype.itemsize for x in list(operands[1:]) + outs)
    return pl.pallas_call(
        kernel,
        out_shape=out_shape,
        in_specs=[smem] + [vmem] * (len(operands) - 1),
        out_specs=[vmem] * len(outs) if isinstance(out_shape, list) else vmem,
        scratch_shapes=list(scratch),
        cost_estimate=pl.CostEstimate(flops=flops, bytes_accessed=moved, transcendentals=0),
        compiler_params=pltpu.CompilerParams(vmem_limit_bytes=12 << 20),
    )(*operands)


def window(place, half):
    return 9 * (place // 2) + 4 * (place % 2) + half


def quad_cut_kernel(me_ref, rows_ref, own_ref, core_ref, chip_ref):
    me = me_ref[0]
    places = ((own_ref, 0), (core_ref, 0), (chip_ref, 0), (chip_ref, 144))
    for step, (out_ref, row) in enumerate(places):
        other = lax.bitwise_xor(me, step)
        for y in range(8):
            start = pl.multiple_of((window(y, 0) + other) * 128, 128)
            out_ref[row : row + 144, y * 256 : (y + 1) * 256] = rows_ref[:, pl.ds(start, 256)]


def quad_cut(me, rows):
    shapes = [jax.ShapeDtypeStruct((count, 2048), BF) for count in (144, 144, 288)]
    return call(quad_cut_kernel, shapes, (me, rows))


def quad_send(piece, step):
    return lax.ppermute(piece, QUAD, [(i, i ^ step) for i in range(4)])


def ring_cut_kernel(me_ref, first_ref, second_ref, *out_refs):
    me = me_ref[0]
    for step, out_ref in enumerate(out_refs):
        other = lax.rem(me + step, 3)
        for g in range(8):
            start = pl.multiple_of((3 * g + other) * 128, 128)
            out_ref[:128, g * 128 : (g + 1) * 128] = first_ref[:, pl.ds(start, 128)]
            out_ref[128:, g * 128 : (g + 1) * 128] = second_ref[:, pl.ds(start, 128)]


def ring_tables(me, first, second):
    pieces = call(ring_cut_kernel, [jax.ShapeDtypeStruct((256, 1024), BF)] * 3, (me, first, second))
    moved = [
        lax.ppermute(pieces[step], "zl", [(i, (i + step) % 3) for i in range(3)]) for step in (1, 2)
    ]
    return [pieces[0]] + moved


def x_kernel(me_ref, held_ref, t0, t1, t2, t3, out_ref, placed):
    me = me_ref[0]
    placed[...] = jnp.zeros_like(placed)
    for y in range(8):
        start = pl.multiple_of(256 * y + 64 * (y % 2) + 16 * me, 16)
        placed[pl.ds(start, 144), :] = held_ref[y]
    for step, table in enumerate((t0, t1, t2, t3)):
        part = jnp.dot(table[:144, :], placed[...], preferred_element_type=F32)
        out_ref[lax.bitwise_xor(me, step)] = part.astype(BF)


def transform_x(me, block, table):
    held = gather(block, "y", 8)
    parts = call(
        x_kernel,
        jax.ShapeDtypeStruct((4, 144, 256), BF),
        (me, held, *table),
        [pltpu.VMEM((2048, 256), BF)],
        flops=2 * 576 * 2048 * 256,
    )
    return scatter_sum(parts, QUAD)


def y_kernel(offset, me_ref, held_ref, t0, t1, t2, out_ref, placed):
    me = me_ref[0]
    for g in range(8):
        placed[:, g * 128 : (g + 1) * 128] = held_ref[g]
    for step, table in enumerate((t0, t1, t2)):
        part = lax.dot_general(
            placed[...],
            table[offset : offset + 128, :],
            (((1,), (1,)), ((), ())),
            preferred_element_type=F32,
        )
        out_ref[lax.rem(me + 3 - step, 3)] = part.astype(BF)


def transform_y(me, block, table, offset):
    held = gather(block, ("xh", "zh"), 8)
    parts = call(
        functools.partial(y_kernel, offset),
        jax.ShapeDtypeStruct((3, 288, 128), BF),
        (me, held, *table),
        [pltpu.VMEM((288, 1024), BF)],
        flops=2 * 288 * 1024 * 384,
    )
    return scatter_sum(parts, "zl")


def to_x(block):
    return jnp.concatenate([block[:144], block[144:]], axis=1)


def to_y(block):
    return jnp.concatenate([block[:, :128], block[:, 128:]], axis=0)


def body(
    u_flow,
    v_flow,
    sea_mask,
    bottom_level,
    mode_project,
    mode_shape,
    forward_x,
    forward_y,
    inverse_x,
    inverse_y,
    eigen_x,
    eigen_y,
    mode_shift,
):
    level_ids = lax.broadcasted_iota(jnp.int32, u_flow.shape, 0)
    wet_int = sea_mask[None] * (level_ids < bottom_level[None]).astype(jnp.int32)
    wet = wet_int.astype(BF)
    flux_u = jnp.einsum("lm,lij->mij", mode_project, u_flow * wet, preferred_element_type=F32)
    flux_v = jnp.einsum("lm,lij->mij", mode_project, v_flow * wet, preferred_element_type=F32)
    flux_u = flux_u.astype(BF).astype(F32)
    flux_v = flux_v.astype(BF).astype(F32)
    mask_f = sea_mask.astype(F32)
    divergence = (mask_f[None] * (centre_x(flux_u) + centre_y(flux_v))).astype(BF)
    quad_me = (lax.axis_index("xl") * 2 + lax.axis_index("c")).astype(jnp.int32).reshape(1)
    ring_me = lax.axis_index("zl").astype(jnp.int32).reshape(1)
    cut_fx = quad_cut(quad_me, forward_x)
    divergence, fx_chip = lax.optimization_barrier((divergence, quad_send(cut_fx[2], 2)))
    table_fx = (cut_fx[0], quad_send(cut_fx[1], 1), fx_chip, quad_send(fx_chip[144:], 1))
    table_y = ring_tables(ring_me, forward_y, inverse_y)
    spec_x = transform_x(quad_me, to_x(divergence.reshape(288, 128)), table_fx).astype(BF)
    spec_x, table_y = lax.optimization_barrier((spec_x, table_y))
    spec_xy = transform_y(ring_me, to_y(spec_x), table_y, 0).reshape(2, 144, 128)
    cut_ix = quad_cut(quad_me, inverse_x)
    spec_xy, ix_chip = lax.optimization_barrier((spec_xy, quad_send(cut_ix[2], 2)))
    denom = eigen_x[None, :, None] + eigen_y[None, None, :] + mode_shift[:, None, None]
    scaled = (spec_xy / denom).astype(BF)
    back_y = transform_y(ring_me, scaled.reshape(288, 128), table_y, 128).astype(BF)
    back_y, ix_one, ix_three = lax.optimization_barrier(
        (back_y, quad_send(cut_ix[1], 1), quad_send(ix_chip[144:], 1))
    )
    table_ix = (cut_ix[0], ix_one, ix_chip, ix_three)
    pressure = to_y(transform_x(quad_me, to_x(back_y), table_ix)).reshape(2, 144, 128)
    grad_x = centre_x(pressure)
    grad_y = centre_y(pressure)
    wet_f = wet_int.astype(F32)
    shape_zero = mode_shape[:, 0][:, None, None]
    shape_one = mode_shape[:, 1][:, None, None]
    u_correct = (-wet_f * (shape_zero * grad_x[0][None] + shape_one * grad_x[1][None])).astype(BF)
    v_correct = (-wet_f * (shape_zero * grad_y[0][None] + shape_one * grad_y[1][None])).astype(BF)
    return (u_correct, v_correct, pressure)


def solution(mesh):
    sub = Mesh(mesh.devices.reshape([n for _, n in SUB]), [name for name, _ in SUB])
    return jax.shard_map(
        body,
        mesh=sub,
        in_specs=(
            P(None, GX, GY),
            P(None, GX, GY),
            P(GX, GY),
            P(GX, GY),
            P(),
            P(),
            P(GX, None),
            P(GY, None),
            P(GX, None),
            P(GY, None),
            P(GX),
            P(GY),
            P(),
        ),
        out_specs=(P(None, GX, GY), P(None, GX, GY), P(None, GX, GY)),
        check_vma=False,
    )
```

```python
import functools

import jax
import jax.numpy as jnp
from jax import lax
from jax.experimental import pallas as pl
from jax.experimental.pallas import tpu as pltpu
from jax.sharding import Mesh
from jax.sharding import PartitionSpec as P

SUB = (("y", 8), ("xl", 2), ("c", 2), ("xh", 2), ("zh", 4), ("zl", 3))
GX = ("y", "xl", "c")
GY = ("xh", "zh", "zl")
QUAD = ("xl", "c")
BF = jnp.bfloat16
F32 = jnp.float32


def gather(block, axes, count):
    return lax.all_to_all(jnp.broadcast_to(block[None], (count,) + block.shape), axes, 0, 0)


def scatter_sum(parts, axes):
    return jnp.sum(lax.all_to_all(parts, axes, 0, 0).astype(F32), axis=0)


def edges(block, axes, dim, count, periodic):
    forward = [(i, i + 1) for i in range(count - 1)]
    if periodic:
        forward.append((count - 1, 0))
    backward = [(target, source) for source, target in forward]
    low = lax.ppermute(lax.slice_in_dim(block, block.shape[dim] - 1, None, axis=dim), axes, forward)
    high = lax.ppermute(lax.slice_in_dim(block, 0, 1, axis=dim), axes, backward)
    return low, high


def centre_x(field):
    low, high = edges(field.astype(BF), GX, 1, 32, True)
    padded = jnp.concatenate([low.astype(F32), field, high.astype(F32)], axis=1)
    return 0.5 * (padded[:, 2:, :] - padded[:, :-2, :])


def centre_y(field):
    low, high = edges(field.astype(BF), GY, 2, 24, False)
    padded = jnp.concatenate([low.astype(F32), field, high.astype(F32)], axis=2)
    return 0.5 * (padded[:, :, 2:] - padded[:, :, :-2])


def call(kernel, out_shape, operands, scratch=(), flops=0):
    smem, vmem = pl.BlockSpec(memory_space=pltpu.SMEM), pl.BlockSpec(memory_space=pltpu.VMEM)
    outs = out_shape if isinstance(out_shape, list) else [out_shape]
    moved = sum(x.size * x.dtype.itemsize for x in list(operands[1:]) + outs)
    return pl.pallas_call(
        kernel,
        out_shape=out_shape,
        in_specs=[smem] + [vmem] * (len(operands) - 1),
        out_specs=[vmem] * len(outs) if isinstance(out_shape, list) else vmem,
        scratch_shapes=list(scratch),
        cost_estimate=pl.CostEstimate(flops=flops, bytes_accessed=moved, transcendentals=0),
        compiler_params=pltpu.CompilerParams(vmem_limit_bytes=12 << 20),
    )(*operands)


def window(place, half):
    return 9 * (place // 2) + 4 * (place % 2) + half


def quad_cut_kernel(me_ref, rows_ref, own_ref, core_ref, chip_ref):
    me = me_ref[0]
    places = ((own_ref, 0), (core_ref, 0), (chip_ref, 0), (chip_ref, 144))
    for step, (out_ref, row) in enumerate(places):
        other = lax.bitwise_xor(me, step)
        for y in range(8):
            start = pl.multiple_of((window(y, 0) + other) * 128, 128)
            out_ref[row : row + 144, y * 256 : (y + 1) * 256] = rows_ref[:, pl.ds(start, 256)]


def quad_cut(me, rows):
    shapes = [jax.ShapeDtypeStruct((count, 2048), BF) for count in (144, 144, 288)]
    return call(quad_cut_kernel, shapes, (me, rows))


def quad_send(piece, step):
    return lax.ppermute(piece, QUAD, [(i, i ^ step) for i in range(4)])


def ring_cut_kernel(me_ref, first_ref, second_ref, *out_refs):
    me = me_ref[0]
    for step, out_ref in enumerate(out_refs):
        other = lax.rem(me + step, 3)
        for g in range(8):
            start = pl.multiple_of((3 * g + other) * 128, 128)
            out_ref[:128, g * 128 : (g + 1) * 128] = first_ref[:, pl.ds(start, 128)]
            out_ref[128:, g * 128 : (g + 1) * 128] = second_ref[:, pl.ds(start, 128)]


def ring_tables(me, first, second):
    pieces = call(ring_cut_kernel, [jax.ShapeDtypeStruct((256, 1024), BF)] * 3, (me, first, second))
    moved = [
        lax.ppermute(pieces[step], "zl", [(i, (i + step) % 3) for i in range(3)]) for step in (1, 2)
    ]
    return [pieces[0]] + moved


def x_kernel(me_ref, held_ref, t0, t1, t2, t3, out_ref, placed):
    me = me_ref[0]
    placed[...] = jnp.zeros_like(placed)
    for y in range(8):
        start = pl.multiple_of(256 * y + 64 * (y % 2) + 16 * me, 16)
        placed[pl.ds(start, 144), :] = held_ref[y]
    for step, table in enumerate((t0, t1, t2, t3)):
        part = jnp.dot(table[:144, :], placed[...], preferred_element_type=F32)
        out_ref[lax.bitwise_xor(me, step)] = part.astype(BF)


def transform_x(me, block, table):
    held = gather(block, "y", 8)
    parts = call(
        x_kernel,
        jax.ShapeDtypeStruct((4, 144, 256), BF),
        (me, held, *table),
        [pltpu.VMEM((2048, 256), BF)],
        flops=2 * 576 * 2048 * 256,
    )
    return scatter_sum(parts, QUAD)


def y_kernel(offset, me_ref, held_ref, t0, t1, t2, out_ref, placed):
    me = me_ref[0]
    for g in range(8):
        placed[:, g * 128 : (g + 1) * 128] = held_ref[g]
    for step, table in enumerate((t0, t1, t2)):
        part = lax.dot_general(
            placed[...],
            table[offset : offset + 128, :],
            (((1,), (1,)), ((), ())),
            preferred_element_type=F32,
        )
        out_ref[lax.rem(me + 3 - step, 3)] = part.astype(BF)


def transform_y(me, block, table, offset):
    held = gather(block, ("xh", "zh"), 8)
    parts = call(
        functools.partial(y_kernel, offset),
        jax.ShapeDtypeStruct((3, 288, 128), BF),
        (me, held, *table),
        [pltpu.VMEM((288, 1024), BF)],
        flops=2 * 288 * 1024 * 384,
    )
    return scatter_sum(parts, "zl")


def nt_dot(left, right):
    return lax.dot_general(left, right, (((1,), (1,)), ((), ())), preferred_element_type=F32)


def x_back_kernel(me_ref, held_ref, t0, t1, t2, t3, lo_ref, hi_ref, out_ref, placed, side, last, first, sums):
    me = me_ref[0]
    placed[...] = jnp.zeros_like(placed)
    sums[...] = jnp.zeros_like(sums)
    for y in range(8):
        shift = 64 * (y % 2) + 16 * me
        placed[pl.ds(pl.multiple_of(256 * y + shift, 16), 144), :] = held_ref[y, :144, :]
        turned = pltpu.roll(held_ref[y, 144:160, :].astype(F32), shift, 1)
        side[:, 256 * y : 256 * (y + 1)] = turned.astype(BF)
    last[0] = jnp.dot(lo_ref[...], placed[...], preferred_element_type=F32)[8:16]
    first[5] = jnp.dot(hi_ref[...], placed[...], preferred_element_type=F32)[:8]
    for step, table in enumerate((t0, t1, t2, t3)):
        target = lax.bitwise_xor(me, step)
        part = jnp.dot(table[:144, :], placed[...], preferred_element_type=F32)
        out_ref[target, :144, :] = part.astype(BF)
        last[target + 1] = part[136:144]
        first[target + 1] = part[:8]
        sums[target, :, :144] = nt_dot(side[...], table[:144, :])
    row = lax.broadcasted_iota(jnp.int32, (16, 256), 0)
    for target in range(4):
        low = jnp.broadcast_to(last[target][7:8], (16, 256))
        high = jnp.broadcast_to(first[target + 2][:1], (16, 256))
        group = jnp.where(row == 2, low, jnp.where(row == 3, high, sums[target]))
        out_ref[target, 144:160, :] = group.astype(BF)


def transform_x_back(me, block, table, outer):
    held = gather(block, "y", 8)
    scratch = [
        pltpu.VMEM((2048, 256), BF),
        pltpu.VMEM((16, 2048), BF),
        pltpu.VMEM((5, 8, 256), F32),
        pltpu.VMEM((6, 8, 256), F32),
        pltpu.VMEM((4, 16, 256), F32),
    ]
    parts = call(
        x_back_kernel,
        jax.ShapeDtypeStruct((4, 160, 256), BF),
        (me, held, *table, *outer),
        scratch,
        flops=2 * 576 * 2048 * 256,
    )
    return scatter_sum(parts, QUAD)


def y_back_kernel(me_ref, held_ref, t0, t1, t2, lo_ref, hi_ref, out_ref, placed, last, first):
    me = me_ref[0]
    placed[288:, :] = jnp.zeros((112, 1024), BF)
    for g in range(8):
        placed[:288, g * 128 : (g + 1) * 128] = held_ref[g]
    last[0] = lo_ref[...]
    first[4] = hi_ref[...]
    for step, table in enumerate((t0, t1, t2)):
        target = lax.rem(me + 3 - step, 3)
        out_ref[target, :288, :] = nt_dot(placed[:288, :], table[128:, :]).astype(BF)
        last[target + 1] = table[240:256, :]
        first[target + 1] = table[128:144, :]
    row = lax.broadcasted_iota(jnp.int32, (16, 128), 0)
    lane = lax.broadcasted_iota(jnp.int32, (32, 128), 1)
    for target in range(3):
        rows = jnp.concatenate([last[target], first[target + 2]], axis=0)
        for mode in range(2):
            head = nt_dot(rows, placed[144 * mode : 144 * mode + 128, :])
            rest = nt_dot(rows, placed[144 * mode + 128 : 144 * mode + 256, :])
            rest = jnp.where(lane < 16, rest, 0.0)
            group = jnp.zeros((16, 128), F32)
            for at, value in ((0, head[15:16]), (1, head[16:17]), (8, rest[15:16]), (9, rest[16:17])):
                group = jnp.where(row == at, jnp.broadcast_to(value, (16, 128)), group)
            out_ref[target, 288 + 16 * mode : 304 + 16 * mode, :] = group.astype(BF)


def transform_y_back(me, block, table, outer):
    held = gather(block, ("xh", "zh"), 8)
    scratch = [
        pltpu.VMEM((400, 1024), BF),
        pltpu.VMEM((4, 16, 1024), BF),
        pltpu.VMEM((5, 16, 1024), BF),
    ]
    parts = call(
        y_back_kernel,
        jax.ShapeDtypeStruct((3, 320, 128), BF),
        (me, held, *table, *outer),
        scratch,
        flops=2 * 288 * 1024 * 384,
    )
    return scatter_sum(parts, "zl")


def ring_outer(me, table):
    low = lax.dynamic_index_in_dim(jnp.stack([t[240:256] for t in table]), (me + 1) % 3, 0, False)
    high = lax.dynamic_index_in_dim(jnp.stack([t[128:144] for t in table]), me, 0, False)
    up = [(i, i + 1) for i in range(7)]
    down = [(i + 1, i) for i in range(7)]
    return lax.ppermute(low, ("xh", "zh"), up), lax.ppermute(high, ("xh", "zh"), down)


def quad_outer(me, table):
    low = lax.dynamic_index_in_dim(jnp.stack([t[128:144] for t in table]), me ^ 3, 0, False)
    high = lax.dynamic_index_in_dim(jnp.stack([t[:16] for t in table]), me, 0, False)
    up = [(i, (i + 1) % 8) for i in range(8)]
    down = [((i + 1) % 8, i) for i in range(8)]
    return lax.ppermute(low, "y", up), lax.ppermute(high, "y", down)


def with_sides(back):
    sides = [
        jnp.concatenate([back[288 + 16 * m : 296 + 16 * m], back[296 + 16 * m : 304 + 16 * m]], axis=1)
        for m in range(2)
    ]
    return jnp.concatenate([to_x(back[:288])] + sides, axis=0)


def to_x(block):
    return jnp.concatenate([block[:144], block[144:]], axis=1)


def to_y(block):
    return jnp.concatenate([block[:, :128], block[:, 128:]], axis=0)


def body(
    u_flow,
    v_flow,
    sea_mask,
    bottom_level,
    mode_project,
    mode_shape,
    forward_x,
    forward_y,
    inverse_x,
    inverse_y,
    eigen_x,
    eigen_y,
    mode_shift,
):
    level_ids = lax.broadcasted_iota(jnp.int32, u_flow.shape, 0)
    wet_int = sea_mask[None] * (level_ids < bottom_level[None]).astype(jnp.int32)
    wet = wet_int.astype(BF)
    flux_u = jnp.einsum("lm,lij->mij", mode_project, u_flow * wet, preferred_element_type=F32)
    flux_v = jnp.einsum("lm,lij->mij", mode_project, v_flow * wet, preferred_element_type=F32)
    flux_u = flux_u.astype(BF).astype(F32)
    flux_v = flux_v.astype(BF).astype(F32)
    mask_f = sea_mask.astype(F32)
    divergence = (mask_f[None] * (centre_x(flux_u) + centre_y(flux_v))).astype(BF)
    quad_me = (lax.axis_index("xl") * 2 + lax.axis_index("c")).astype(jnp.int32).reshape(1)
    ring_me = lax.axis_index("zl").astype(jnp.int32).reshape(1)
    cut_fx = quad_cut(quad_me, forward_x)
    divergence, fx_chip = lax.optimization_barrier((divergence, quad_send(cut_fx[2], 2)))
    table_fx = (cut_fx[0], quad_send(cut_fx[1], 1), fx_chip, quad_send(fx_chip[144:], 1))
    table_y = ring_tables(ring_me, forward_y, inverse_y)
    spec_x = transform_x(quad_me, to_x(divergence.reshape(288, 128)), table_fx).astype(BF)
    spec_x, table_y = lax.optimization_barrier((spec_x, table_y))
    spec_xy = transform_y(ring_me, to_y(spec_x), table_y, 0).reshape(2, 144, 128)
    cut_ix = quad_cut(quad_me, inverse_x)
    spec_xy, ix_chip = lax.optimization_barrier((spec_xy, quad_send(cut_ix[2], 2)))
    denom = eigen_x[None, :, None] + eigen_y[None, None, :] + mode_shift[:, None, None]
    scaled = (spec_xy / denom).astype(BF)
    outer_y = ring_outer(ring_me[0], table_y)
    back_y = transform_y_back(ring_me, scaled.reshape(288, 128), table_y, outer_y).astype(BF)
    back_y, ix_one, ix_three = lax.optimization_barrier(
        (back_y, quad_send(cut_ix[1], 1), quad_send(ix_chip[144:], 1))
    )
    table_ix = (cut_ix[0], ix_one, ix_chip, ix_three)
    outer_x = quad_outer(quad_me[0], table_ix)
    total = transform_x_back(quad_me, with_sides(back_y), table_ix, outer_x)
    pressure = to_y(total[:144]).reshape(2, 144, 128)
    low, high = total[146].reshape(2, 1, 128), total[147].reshape(2, 1, 128)
    padded = jnp.concatenate([low, pressure, high], axis=1)
    grad_x = 0.5 * (padded[:, 2:, :] - padded[:, :-2, :])
    sides = jnp.stack([total[144:146, :144], total[152:154, :144]])
    padded = jnp.concatenate([sides[:, 0, :, None], pressure, sides[:, 1, :, None]], axis=2)
    grad_y = 0.5 * (padded[:, :, 2:] - padded[:, :, :-2])
    wet_f = wet_int.astype(F32)
    shape_zero = mode_shape[:, 0][:, None, None]
    shape_one = mode_shape[:, 1][:, None, None]
    u_correct = (-wet_f * (shape_zero * grad_x[0][None] + shape_one * grad_x[1][None])).astype(BF)
    v_correct = (-wet_f * (shape_zero * grad_y[0][None] + shape_one * grad_y[1][None])).astype(BF)
    return (u_correct, v_correct, pressure)


def solution(mesh):
    sub = Mesh(mesh.devices.reshape([n for _, n in SUB]), [name for name, _ in SUB])
    return jax.shard_map(
        body,
        mesh=sub,
        in_specs=(
            P(None, GX, GY),
            P(None, GX, GY),
            P(GX, GY),
            P(GX, GY),
            P(),
            P(),
            P(GX, None),
            P(GY, None),
            P(GX, None),
            P(GY, None),
            P(GX),
            P(GY),
            P(),
        ),
        out_specs=(P(None, GX, GY), P(None, GX, GY), P(None, GX, GY)),
        check_vma=False,
    )
```

```python
import functools

import jax
import jax.numpy as jnp
from jax import lax
from jax.experimental import pallas as pl
from jax.experimental.pallas import tpu as pltpu
from jax.sharding import Mesh
from jax.sharding import PartitionSpec as P

SUB = (("y", 8), ("xl", 2), ("c", 2), ("xh", 2), ("zh", 4), ("zl", 3))
GX = ("y", "xl", "c")
GY = ("xh", "zh", "zl")
QUAD = ("xl", "c")
BF = jnp.bfloat16
F32 = jnp.float32


def gather(block, axes, count):
    return lax.all_to_all(jnp.broadcast_to(block[None], (count,) + block.shape), axes, 0, 0)


def scatter_sum(parts, axes):
    return jnp.sum(lax.all_to_all(parts, axes, 0, 0).astype(F32), axis=0)


def edges(block, axes, dim, count, periodic):
    forward = [(i, i + 1) for i in range(count - 1)]
    if periodic:
        forward.append((count - 1, 0))
    backward = [(target, source) for source, target in forward]
    low = lax.ppermute(lax.slice_in_dim(block, block.shape[dim] - 1, None, axis=dim), axes, forward)
    high = lax.ppermute(lax.slice_in_dim(block, 0, 1, axis=dim), axes, backward)
    return low, high


def centre_x(field):
    low, high = edges(field.astype(BF), GX, 1, 32, True)
    padded = jnp.concatenate([low.astype(F32), field, high.astype(F32)], axis=1)
    return 0.5 * (padded[:, 2:, :] - padded[:, :-2, :])


def centre_y(field):
    low, high = edges(field.astype(BF), GY, 2, 24, False)
    padded = jnp.concatenate([low.astype(F32), field, high.astype(F32)], axis=2)
    return 0.5 * (padded[:, :, 2:] - padded[:, :, :-2])


def call(kernel, out_shape, operands, scratch=(), flops=0):
    smem, vmem = pl.BlockSpec(memory_space=pltpu.SMEM), pl.BlockSpec(memory_space=pltpu.VMEM)
    outs = out_shape if isinstance(out_shape, list) else [out_shape]
    moved = sum(x.size * x.dtype.itemsize for x in list(operands[1:]) + outs)
    return pl.pallas_call(
        kernel,
        out_shape=out_shape,
        in_specs=[smem] + [vmem] * (len(operands) - 1),
        out_specs=[vmem] * len(outs) if isinstance(out_shape, list) else vmem,
        scratch_shapes=list(scratch),
        cost_estimate=pl.CostEstimate(flops=flops, bytes_accessed=moved, transcendentals=0),
        compiler_params=pltpu.CompilerParams(vmem_limit_bytes=12 << 20),
    )(*operands)


def window(place, half):
    return 9 * (place // 2) + 4 * (place % 2) + half


def quad_cut_kernel(me_ref, rows_ref, *out_refs):
    me = me_ref[0]
    for step, out_ref in enumerate(out_refs):
        other = lax.bitwise_xor(me, step)
        for y in range(8):
            start = pl.multiple_of((window(y, 0) + other) * 128, 128)
            back = lax.rem(256 - 64 * (y % 2) - 16 * other, 256)
            packed = pltpu.roll(rows_ref[:, pl.ds(start, 256)].astype(F32), back, 1)
            out_ref[:, 144 * y : 144 * (y + 1)] = packed[:, :144].astype(BF)


def quad_cut(me, rows):
    return call(quad_cut_kernel, [jax.ShapeDtypeStruct((144, 1152), BF)] * 4, (me, rows))


def quad_send(piece, step):
    return lax.ppermute(piece, QUAD, [(i, i ^ step) for i in range(4)])


def ring_cut_kernel(me_ref, first_ref, second_ref, *out_refs):
    me = me_ref[0]
    for step, out_ref in enumerate(out_refs):
        other = lax.rem(me + step, 3)
        for g in range(8):
            start = pl.multiple_of((3 * g + other) * 128, 128)
            out_ref[:128, g * 128 : (g + 1) * 128] = first_ref[:, pl.ds(start, 128)]
            out_ref[128:, g * 128 : (g + 1) * 128] = second_ref[:, pl.ds(start, 128)]


def ring_cut(me, first, second):
    return call(ring_cut_kernel, [jax.ShapeDtypeStruct((256, 1024), BF)] * 3, (me, first, second))


def ring_tables(pieces):
    moved = [
        lax.ppermute(pieces[step], "zl", [(i, (i + step) % 3) for i in range(3)]) for step in (1, 2)
    ]
    return [pieces[0]] + moved


def x_kernel(me_ref, held_ref, t0, t1, t2, t3, out_ref):
    me = me_ref[0]
    for step, table in enumerate((t0, t1, t2, t3)):
        part = jnp.dot(table[...], held_ref[...], preferred_element_type=F32)
        out_ref[lax.bitwise_xor(me, step)] = part.astype(BF)


def transform_x(me, block, table):
    held = gather(block, "y", 8).reshape(1152, 256)
    parts = call(
        x_kernel,
        jax.ShapeDtypeStruct((4, 144, 256), BF),
        (me, held, *table),
        flops=2 * 576 * 1152 * 256,
    )
    return scatter_sum(parts, QUAD)


def y_kernel(offset, me_ref, held_ref, t0, t1, t2, out_ref, placed):
    me = me_ref[0]
    for g in range(8):
        placed[:, g * 128 : (g + 1) * 128] = held_ref[g]
    for step, table in enumerate((t0, t1, t2)):
        part = lax.dot_general(
            placed[...],
            table[offset : offset + 128, :],
            (((1,), (1,)), ((), ())),
            preferred_element_type=F32,
        )
        out_ref[lax.rem(me + 3 - step, 3)] = part.astype(BF)


def transform_y(me, block, table, offset):
    held = gather(block, ("xh", "zh"), 8)
    parts = call(
        functools.partial(y_kernel, offset),
        jax.ShapeDtypeStruct((3, 288, 128), BF),
        (me, held, *table),
        [pltpu.VMEM((288, 1024), BF)],
        flops=2 * 288 * 1024 * 384,
    )
    return scatter_sum(parts, "zl")


def nt_dot(left, right):
    return lax.dot_general(left, right, (((1,), (1,)), ((), ())), preferred_element_type=F32)


def x_back_kernel(me_ref, held_ref, t0, t1, t2, t3, lo_ref, hi_ref, out_ref, placed, side, last, first, sums):
    me = me_ref[0]
    sums[...] = jnp.zeros_like(sums)
    for y in range(8):
        placed[144 * y : 144 * (y + 1), :] = held_ref[y, :144, :]
        side[:, 144 * y : 144 * (y + 1)] = held_ref[y, 144:160, :144]
    last[0] = jnp.dot(lo_ref[...], placed[...], preferred_element_type=F32)[8:16]
    first[5] = jnp.dot(hi_ref[...], placed[...], preferred_element_type=F32)[:8]
    for step, table in enumerate((t0, t1, t2, t3)):
        target = lax.bitwise_xor(me, step)
        part = jnp.dot(table[...], placed[...], preferred_element_type=F32)
        out_ref[target, :144, :] = part.astype(BF)
        last[target + 1] = part[136:144]
        first[target + 1] = part[:8]
        sums[target, :, :144] = nt_dot(side[...], table[...])
    row = lax.broadcasted_iota(jnp.int32, (16, 256), 0)
    for target in range(4):
        low = jnp.broadcast_to(last[target][7:8], (16, 256))
        high = jnp.broadcast_to(first[target + 2][:1], (16, 256))
        group = jnp.where(row == 2, low, jnp.where(row == 3, high, sums[target]))
        out_ref[target, 144:160, :] = group.astype(BF)


def transform_x_back(me, block, table, outer):
    held = gather(block, "y", 8)
    scratch = [
        pltpu.VMEM((1152, 256), BF),
        pltpu.VMEM((16, 1152), BF),
        pltpu.VMEM((5, 8, 256), F32),
        pltpu.VMEM((6, 8, 256), F32),
        pltpu.VMEM((4, 16, 256), F32),
    ]
    parts = call(
        x_back_kernel,
        jax.ShapeDtypeStruct((4, 160, 256), BF),
        (me, held, *table, *outer),
        scratch,
        flops=2 * 576 * 1152 * 256,
    )
    return scatter_sum(parts, QUAD)


def y_back_kernel(me_ref, held_ref, t0, t1, t2, lo_ref, hi_ref, out_ref, placed, last, first):
    me = me_ref[0]
    placed[288:, :] = jnp.zeros((112, 1024), BF)
    for g in range(8):
        placed[:288, g * 128 : (g + 1) * 128] = held_ref[g]
    last[0] = lo_ref[...]
    first[4] = hi_ref[...]
    for step, table in enumerate((t0, t1, t2)):
        target = lax.rem(me + 3 - step, 3)
        out_ref[target, :288, :] = nt_dot(placed[:288, :], table[128:, :]).astype(BF)
        last[target + 1] = table[240:256, :]
        first[target + 1] = table[128:144, :]
    row = lax.broadcasted_iota(jnp.int32, (16, 128), 0)
    lane = lax.broadcasted_iota(jnp.int32, (32, 128), 1)
    for target in range(3):
        rows = jnp.concatenate([last[target], first[target + 2]], axis=0)
        for mode in range(2):
            head = nt_dot(rows, placed[144 * mode : 144 * mode + 128, :])
            rest = nt_dot(rows, placed[144 * mode + 128 : 144 * mode + 256, :])
            rest = jnp.where(lane < 16, rest, 0.0)
            group = jnp.zeros((16, 128), F32)
            for at, value in ((0, head[15:16]), (1, head[16:17]), (8, rest[15:16]), (9, rest[16:17])):
                group = jnp.where(row == at, jnp.broadcast_to(value, (16, 128)), group)
            out_ref[target, 288 + 16 * mode : 304 + 16 * mode, :] = group.astype(BF)


def transform_y_back(me, block, table, outer):
    held = gather(block, ("xh", "zh"), 8)
    scratch = [
        pltpu.VMEM((400, 1024), BF),
        pltpu.VMEM((4, 16, 1024), BF),
        pltpu.VMEM((5, 16, 1024), BF),
    ]
    parts = call(
        y_back_kernel,
        jax.ShapeDtypeStruct((3, 320, 128), BF),
        (me, held, *table, *outer),
        scratch,
        flops=2 * 288 * 1024 * 384,
    )
    return scatter_sum(parts, "zl")


def ring_outer(me, table):
    low = lax.dynamic_index_in_dim(jnp.stack([t[240:256] for t in table]), (me + 1) % 3, 0, False)
    high = lax.dynamic_index_in_dim(jnp.stack([t[128:144] for t in table]), me, 0, False)
    up = [(i, i + 1) for i in range(7)]
    down = [(i + 1, i) for i in range(7)]
    return lax.ppermute(low, ("xh", "zh"), up), lax.ppermute(high, ("xh", "zh"), down)


def quad_outer(me, table):
    low = lax.dynamic_index_in_dim(jnp.stack([t[128:144] for t in table]), me ^ 3, 0, False)
    high = lax.dynamic_index_in_dim(jnp.stack([t[:16] for t in table]), me, 0, False)
    up = [(i, (i + 1) % 8) for i in range(8)]
    down = [((i + 1) % 8, i) for i in range(8)]
    return lax.ppermute(low, "y", up), lax.ppermute(high, "y", down)


def with_sides(back):
    sides = [
        jnp.concatenate([back[288 + 16 * m : 296 + 16 * m], back[296 + 16 * m : 304 + 16 * m]], axis=1)
        for m in range(2)
    ]
    return jnp.concatenate([to_x(back[:288])] + sides, axis=0)


def to_x(block):
    return jnp.concatenate([block[:144], block[144:]], axis=1)


def to_y(block):
    return jnp.concatenate([block[:, :128], block[:, 128:]], axis=0)


def body(
    u_flow,
    v_flow,
    sea_mask,
    bottom_level,
    mode_project,
    mode_shape,
    forward_x,
    forward_y,
    inverse_x,
    inverse_y,
    eigen_x,
    eigen_y,
    mode_shift,
):
    level_ids = lax.broadcasted_iota(jnp.int32, u_flow.shape, 0)
    wet_int = sea_mask[None] * (level_ids < bottom_level[None]).astype(jnp.int32)
    wet = wet_int.astype(BF)
    flux_u = jnp.einsum("lm,lij->mij", mode_project, u_flow * wet, preferred_element_type=F32)
    flux_v = jnp.einsum("lm,lij->mij", mode_project, v_flow * wet, preferred_element_type=F32)
    flux_u = flux_u.astype(BF).astype(F32)
    flux_v = flux_v.astype(BF).astype(F32)
    mask_f = sea_mask.astype(F32)
    divergence = (mask_f[None] * (centre_x(flux_u) + centre_y(flux_v))).astype(BF)
    quad_me = (lax.axis_index("xl") * 2 + lax.axis_index("c")).astype(jnp.int32).reshape(1)
    ring_me = lax.axis_index("zl").astype(jnp.int32).reshape(1)
    cut_fx, cut_y = quad_cut(quad_me, forward_x), ring_cut(ring_me, forward_y, inverse_y)
    divergence, cut_fx, cut_y = lax.optimization_barrier((divergence, cut_fx, cut_y))
    table_fx = [cut_fx[0]] + [quad_send(cut_fx[step], step) for step in (1, 2, 3)]
    table_y = ring_tables(cut_y)
    spec_x = transform_x(quad_me, to_x(divergence.reshape(288, 128)), table_fx).astype(BF)
    spec_x, table_y = lax.optimization_barrier((spec_x, table_y))
    spec_xy = transform_y(ring_me, to_y(spec_x), table_y, 0).reshape(2, 144, 128)
    cut_ix = quad_cut(quad_me, inverse_x)
    spec_xy, ix_two = lax.optimization_barrier((spec_xy, quad_send(cut_ix[2], 2)))
    denom = eigen_x[None, :, None] + eigen_y[None, None, :] + mode_shift[:, None, None]
    scaled = (spec_xy / denom).astype(BF)
    outer_y = ring_outer(ring_me[0], table_y)
    back_y = transform_y_back(ring_me, scaled.reshape(288, 128), table_y, outer_y).astype(BF)
    back_y, ix_one, ix_three = lax.optimization_barrier(
        (back_y, quad_send(cut_ix[1], 1), quad_send(cut_ix[3], 3))
    )
    table_ix = (cut_ix[0], ix_one, ix_two, ix_three)
    outer_x = quad_outer(quad_me[0], table_ix)
    total = transform_x_back(quad_me, with_sides(back_y), table_ix, outer_x)
    pressure = to_y(total[:144]).reshape(2, 144, 128)
    low, high = total[146].reshape(2, 1, 128), total[147].reshape(2, 1, 128)
    padded = jnp.concatenate([low, pressure, high], axis=1)
    grad_x = 0.5 * (padded[:, 2:, :] - padded[:, :-2, :])
    sides = jnp.stack([total[144:146, :144], total[152:154, :144]])
    padded = jnp.concatenate([sides[:, 0, :, None], pressure, sides[:, 1, :, None]], axis=2)
    grad_y = 0.5 * (padded[:, :, 2:] - padded[:, :, :-2])
    wet_f = wet_int.astype(F32)
    shape_zero = mode_shape[:, 0][:, None, None]
    shape_one = mode_shape[:, 1][:, None, None]
    u_correct = (-wet_f * (shape_zero * grad_x[0][None] + shape_one * grad_x[1][None])).astype(BF)
    v_correct = (-wet_f * (shape_zero * grad_y[0][None] + shape_one * grad_y[1][None])).astype(BF)
    return (u_correct, v_correct, pressure)


def solution(mesh):
    sub = Mesh(mesh.devices.reshape([n for _, n in SUB]), [name for name, _ in SUB])
    return jax.shard_map(
        body,
        mesh=sub,
        in_specs=(
            P(None, GX, GY),
            P(None, GX, GY),
            P(GX, GY),
            P(GX, GY),
            P(),
            P(),
            P(GX, None),
            P(GY, None),
            P(GX, None),
            P(GY, None),
            P(GX),
            P(GY),
            P(),
        ),
        out_specs=(P(None, GX, GY), P(None, GX, GY), P(None, GX, GY)),
        check_vma=False,
    )
```

```python
import functools

import jax
import jax.numpy as jnp
from jax import lax
from jax.experimental import pallas as pl
from jax.experimental.pallas import tpu as pltpu
from jax.sharding import Mesh
from jax.sharding import PartitionSpec as P

SUB = (("y", 8), ("xl", 2), ("c", 2), ("xh", 2), ("zh", 4), ("zl", 3))
GX = ("y", "xl", "c")
GY = ("xh", "zh", "zl")
QUAD = ("xl", "c")
BF = jnp.bfloat16
F32 = jnp.float32


def exchange(parts, axes):
    return lax.all_to_all(parts, axes, 0, 0)


def edges(block, axes, dim, count, periodic):
    forward = [(i, i + 1) for i in range(count - 1)]
    if periodic:
        forward.append((count - 1, 0))
    backward = [(target, source) for source, target in forward]
    low = lax.ppermute(lax.slice_in_dim(block, block.shape[dim] - 1, None, axis=dim), axes, forward)
    high = lax.ppermute(lax.slice_in_dim(block, 0, 1, axis=dim), axes, backward)
    return low, high


def centre_x(field):
    low, high = edges(field.astype(BF), GX, 1, 32, True)
    padded = jnp.concatenate([low.astype(F32), field, high.astype(F32)], axis=1)
    return 0.5 * (padded[:, 2:, :] - padded[:, :-2, :])


def centre_y(field):
    low, high = edges(field.astype(BF), GY, 2, 24, False)
    padded = jnp.concatenate([low.astype(F32), field, high.astype(F32)], axis=2)
    return 0.5 * (padded[:, :, 2:] - padded[:, :, :-2])


def call(kernel, out_shape, operands, scratch=(), flops=0):
    smem, vmem = pl.BlockSpec(memory_space=pltpu.SMEM), pl.BlockSpec(memory_space=pltpu.VMEM)
    outs = out_shape if isinstance(out_shape, list) else [out_shape]
    moved = sum(x.size * x.dtype.itemsize for x in list(operands[1:]) + outs)
    return pl.pallas_call(
        kernel,
        out_shape=out_shape,
        in_specs=[smem] + [vmem] * (len(operands) - 1),
        out_specs=[vmem] * len(outs) if isinstance(out_shape, list) else vmem,
        scratch_shapes=list(scratch),
        cost_estimate=pl.CostEstimate(flops=flops, bytes_accessed=moved, transcendentals=0),
        compiler_params=pltpu.CompilerParams(vmem_limit_bytes=12 << 20),
    )(*operands)


def window(place, half):
    return 9 * (place // 2) + 4 * (place % 2) + half


def quad_cut_kernel(me_ref, rows_ref, *out_refs):
    me = me_ref[0]
    for step, out_ref in enumerate(out_refs):
        other = lax.bitwise_xor(me, step)
        for y in range(8):
            start = pl.multiple_of((window(y, 0) + other) * 128, 128)
            back = lax.rem(256 - 64 * (y % 2) - 16 * other, 256)
            packed = pltpu.roll(rows_ref[:, pl.ds(start, 256)].astype(F32), back, 1)
            out_ref[:, 144 * y : 144 * (y + 1)] = packed[:, :144].astype(BF)


def quad_cut(me, rows):
    return call(quad_cut_kernel, [jax.ShapeDtypeStruct((144, 1152), BF)] * 4, (me, rows))


def quad_send(piece, step):
    return lax.ppermute(piece, QUAD, [(i, i ^ step) for i in range(4)])


def ring_cut_kernel(me_ref, first_ref, second_ref, *out_refs):
    me = me_ref[0]
    for step, out_ref in enumerate(out_refs):
        other = lax.rem(me + step, 3)
        for g in range(8):
            start = pl.multiple_of((3 * g + other) * 128, 128)
            out_ref[:128, g * 128 : (g + 1) * 128] = first_ref[:, pl.ds(start, 128)]
            out_ref[128:, g * 128 : (g + 1) * 128] = second_ref[:, pl.ds(start, 128)]


def ring_cut(me, first, second):
    return call(ring_cut_kernel, [jax.ShapeDtypeStruct((256, 1024), BF)] * 3, (me, first, second))


def ring_tables(pieces):
    moved = [
        lax.ppermute(pieces[step], "zl", [(i, (i + step) % 3) for i in range(3)]) for step in (1, 2)
    ]
    return [pieces[0]] + moved


def x_kernel(me_ref, held_ref, t0, t1, t2, t3, out_ref):
    me = me_ref[0]
    for step, table in enumerate((t0, t1, t2, t3)):
        part = jnp.dot(table[...], held_ref[...], preferred_element_type=F32)
        out_ref[lax.bitwise_xor(me, step)] = part.astype(BF)


def x_products(me, held, table):
    held = held.reshape(1152, 256)
    out = jax.ShapeDtypeStruct((4, 144, 256), BF)
    return call(x_kernel, out, (me, held, *table), flops=2 * 576 * 1152 * 256)


def y_kernel(offset, me_ref, held_ref, t0, t1, t2, out_ref, placed):
    me = me_ref[0]
    for g in range(8):
        placed[:, g * 128 : (g + 1) * 128] = held_ref[g]
    for step, table in enumerate((t0, t1, t2)):
        part = lax.dot_general(
            placed[...],
            table[offset : offset + 128, :],
            (((1,), (1,)), ((), ())),
            preferred_element_type=F32,
        )
        out_ref[lax.rem(me + 3 - step, 3)] = part.astype(BF)


def y_products(me, held, table):
    out = jax.ShapeDtypeStruct((3, 288, 128), BF)
    scratch = [pltpu.VMEM((288, 1024), BF)]
    return call(functools.partial(y_kernel, 0), out, (me, held, *table), scratch, flops=2 * 288 * 1024 * 384)


def added(got_ref):
    total = got_ref[0].astype(F32)
    for source in range(1, got_ref.shape[0]):
        total = total + got_ref[source].astype(F32)
    return total


def to_y_kernel(me_ref, got_ref, out_ref):
    total = added(got_ref).astype(BF)
    for g in range(8):
        out_ref[g, :144, :] = total[:, :128]
        out_ref[g, 144:, :] = total[:, 128:]


def scale_kernel(shift_ref, got_ref, x_ref, y_ref, out_ref):
    total = added(got_ref)
    denom = x_ref[...] + y_ref[...]
    for mode in range(2):
        rows = slice(144 * mode, 144 * (mode + 1))
        scaled = (total[rows] / (denom + shift_ref[mode])).astype(BF)
        for g in range(8):
            out_ref[g, rows, :] = scaled


def to_x_kernel(me_ref, got_ref, out_ref):
    total = added(got_ref)
    main = total[:288].astype(BF)
    sides = jnp.concatenate(
        [
            jnp.concatenate([total[288:296], total[304:312]], axis=0),
            jnp.concatenate([total[296:304], total[312:320]], axis=0),
        ],
        axis=1,
    ).astype(BF)
    for g in range(8):
        out_ref[g, :144, :128] = main[:144]
        out_ref[g, :144, 128:] = main[144:]
        out_ref[g, 144:, :] = sides


def nt_dot(left, right):
    return lax.dot_general(left, right, (((1,), (1,)), ((), ())), preferred_element_type=F32)


def x_back_kernel(me_ref, held_ref, t0, t1, t2, t3, lo_ref, hi_ref, out_ref, placed, side, last, first, sums):
    me = me_ref[0]
    sums[...] = jnp.zeros_like(sums)
    for y in range(8):
        placed[144 * y : 144 * (y + 1), :] = held_ref[y, :144, :]
        side[:, 144 * y : 144 * (y + 1)] = held_ref[y, 144:160, :144]
    last[0] = jnp.dot(lo_ref[...], placed[...], preferred_element_type=F32)[8:16]
    first[5] = jnp.dot(hi_ref[...], placed[...], preferred_element_type=F32)[:8]
    for step, table in enumerate((t0, t1, t2, t3)):
        target = lax.bitwise_xor(me, step)
        part = jnp.dot(table[...], placed[...], preferred_element_type=F32)
        out_ref[target, :144, :] = part.astype(BF)
        last[target + 1] = part[136:144]
        first[target + 1] = part[:8]
        sums[target, :, :144] = nt_dot(side[...], table[...])
    row = lax.broadcasted_iota(jnp.int32, (16, 256), 0)
    for target in range(4):
        low = jnp.broadcast_to(last[target][7:8], (16, 256))
        high = jnp.broadcast_to(first[target + 2][:1], (16, 256))
        group = jnp.where(row == 2, low, jnp.where(row == 3, high, sums[target]))
        out_ref[target, 144:160, :] = group.astype(BF)


def x_back_products(me, held, table, outer):
    scratch = [
        pltpu.VMEM((1152, 256), BF),
        pltpu.VMEM((16, 1152), BF),
        pltpu.VMEM((5, 8, 256), F32),
        pltpu.VMEM((6, 8, 256), F32),
        pltpu.VMEM((4, 16, 256), F32),
    ]
    out = jax.ShapeDtypeStruct((4, 160, 256), BF)
    return call(x_back_kernel, out, (me, held, *table, *outer), scratch, flops=2 * 576 * 1152 * 256)


def y_back_kernel(me_ref, held_ref, t0, t1, t2, lo_ref, hi_ref, out_ref, placed, last, first):
    me = me_ref[0]
    placed[288:, :] = jnp.zeros((112, 1024), BF)
    for g in range(8):
        placed[:288, g * 128 : (g + 1) * 128] = held_ref[g]
    last[0] = lo_ref[...]
    first[4] = hi_ref[...]
    for step, table in enumerate((t0, t1, t2)):
        target = lax.rem(me + 3 - step, 3)
        out_ref[target, :288, :] = nt_dot(placed[:288, :], table[128:, :]).astype(BF)
        last[target + 1] = table[240:256, :]
        first[target + 1] = table[128:144, :]
    row = lax.broadcasted_iota(jnp.int32, (16, 128), 0)
    lane = lax.broadcasted_iota(jnp.int32, (32, 128), 1)
    for target in range(3):
        rows = jnp.concatenate([last[target], first[target + 2]], axis=0)
        for mode in range(2):
            head = nt_dot(rows, placed[144 * mode : 144 * mode + 128, :])
            rest = nt_dot(rows, placed[144 * mode + 128 : 144 * mode + 256, :])
            rest = jnp.where(lane < 16, rest, 0.0)
            group = jnp.zeros((16, 128), F32)
            for at, value in ((0, head[15:16]), (1, head[16:17]), (8, rest[15:16]), (9, rest[16:17])):
                group = jnp.where(row == at, jnp.broadcast_to(value, (16, 128)), group)
            out_ref[target, 288 + 16 * mode : 304 + 16 * mode, :] = group.astype(BF)


def y_back_products(me, held, table, outer):
    scratch = [
        pltpu.VMEM((400, 1024), BF),
        pltpu.VMEM((4, 16, 1024), BF),
        pltpu.VMEM((5, 16, 1024), BF),
    ]
    out = jax.ShapeDtypeStruct((3, 320, 128), BF)
    return call(y_back_kernel, out, (me, held, *table, *outer), scratch, flops=2 * 288 * 1024 * 384)


def ring_outer(me, table):
    low = lax.dynamic_index_in_dim(jnp.stack([t[240:256] for t in table]), (me + 1) % 3, 0, False)
    high = lax.dynamic_index_in_dim(jnp.stack([t[128:144] for t in table]), me, 0, False)
    up = [(i, i + 1) for i in range(7)]
    down = [(i + 1, i) for i in range(7)]
    return lax.ppermute(low, ("xh", "zh"), up), lax.ppermute(high, ("xh", "zh"), down)


def quad_outer(me, table):
    low = lax.dynamic_index_in_dim(jnp.stack([t[128:144] for t in table]), me ^ 3, 0, False)
    high = lax.dynamic_index_in_dim(jnp.stack([t[:16] for t in table]), me, 0, False)
    up = [(i, (i + 1) % 8) for i in range(8)]
    down = [((i + 1) % 8, i) for i in range(8)]
    return lax.ppermute(low, "y", up), lax.ppermute(high, "y", down)


def to_x(block):
    return jnp.concatenate([block[:144], block[144:]], axis=1)


def to_y(block):
    return jnp.concatenate([block[:, :128], block[:, 128:]], axis=0)


def body(
    u_flow,
    v_flow,
    sea_mask,
    bottom_level,
    mode_project,
    mode_shape,
    forward_x,
    forward_y,
    inverse_x,
    inverse_y,
    eigen_x,
    eigen_y,
    mode_shift,
):
    level_ids = lax.broadcasted_iota(jnp.int32, u_flow.shape, 0)
    wet_int = sea_mask[None] * (level_ids < bottom_level[None]).astype(jnp.int32)
    wet = wet_int.astype(BF)
    flux_u = jnp.einsum("lm,lij->mij", mode_project, u_flow * wet, preferred_element_type=F32)
    flux_v = jnp.einsum("lm,lij->mij", mode_project, v_flow * wet, preferred_element_type=F32)
    flux_u = flux_u.astype(BF).astype(F32)
    flux_v = flux_v.astype(BF).astype(F32)
    mask_f = sea_mask.astype(F32)
    divergence = (mask_f[None] * (centre_x(flux_u) + centre_y(flux_v))).astype(BF)
    quad_me = (lax.axis_index("xl") * 2 + lax.axis_index("c")).astype(jnp.int32).reshape(1)
    ring_me = lax.axis_index("zl").astype(jnp.int32).reshape(1)
    cut_fx, cut_y = quad_cut(quad_me, forward_x), ring_cut(ring_me, forward_y, inverse_y)
    divergence, fx_two, cut_y = lax.optimization_barrier((divergence, quad_send(cut_fx[2], 2), cut_y))
    table_fx = (cut_fx[0], quad_send(cut_fx[1], 1), fx_two, quad_send(cut_fx[3], 3))
    table_y = ring_tables(cut_y)
    block = to_x(divergence.reshape(288, 128))
    held = exchange(jnp.broadcast_to(block[None], (8, 144, 256)), "y")
    got = exchange(x_products(quad_me, held, table_fx), QUAD)
    got, table_y = lax.optimization_barrier((got, table_y))
    spread = jax.ShapeDtypeStruct((8, 288, 128), BF)
    held = exchange(call(to_y_kernel, spread, (quad_me, got)), ("xh", "zh"))
    cut_ix = quad_cut(quad_me, inverse_x)
    held, table_ix = lax.optimization_barrier(
        (held, [cut_ix[0]] + [quad_send(cut_ix[step], step) for step in (1, 2, 3)])
    )
    got = exchange(y_products(ring_me, held, table_y), "zl")
    eigen = (eigen_x.reshape(144, 1), eigen_y.reshape(1, 128))
    held = exchange(call(scale_kernel, spread, (mode_shift, got, *eigen)), ("xh", "zh"))
    outer_y, outer_x = ring_outer(ring_me[0], table_y), quad_outer(quad_me[0], table_ix)
    held, outer_x = lax.optimization_barrier((held, outer_x))
    got = exchange(y_back_products(ring_me, held, table_y, outer_y), "zl")
    spread = jax.ShapeDtypeStruct((8, 160, 256), BF)
    held = exchange(call(to_x_kernel, spread, (quad_me, got)), "y")
    parts = exchange(x_back_products(quad_me, held, table_ix, outer_x), QUAD)
    total = jnp.sum(parts.astype(F32), axis=0)
    pressure = to_y(total[:144]).reshape(2, 144, 128)
    low, high = total[146].reshape(2, 1, 128), total[147].reshape(2, 1, 128)
    padded = jnp.concatenate([low, pressure, high], axis=1)
    grad_x = 0.5 * (padded[:, 2:, :] - padded[:, :-2, :])
    sides = jnp.stack([total[144:146, :144], total[152:154, :144]])
    padded = jnp.concatenate([sides[:, 0, :, None], pressure, sides[:, 1, :, None]], axis=2)
    grad_y = 0.5 * (padded[:, :, 2:] - padded[:, :, :-2])
    wet_f = wet_int.astype(F32)
    shape_zero = mode_shape[:, 0][:, None, None]
    shape_one = mode_shape[:, 1][:, None, None]
    u_correct = (-wet_f * (shape_zero * grad_x[0][None] + shape_one * grad_x[1][None])).astype(BF)
    v_correct = (-wet_f * (shape_zero * grad_y[0][None] + shape_one * grad_y[1][None])).astype(BF)
    return (u_correct, v_correct, pressure)


def solution(mesh):
    sub = Mesh(mesh.devices.reshape([n for _, n in SUB]), [name for name, _ in SUB])
    return jax.shard_map(
        body,
        mesh=sub,
        in_specs=(
            P(None, GX, GY),
            P(None, GX, GY),
            P(GX, GY),
            P(GX, GY),
            P(),
            P(),
            P(GX, None),
            P(GY, None),
            P(GX, None),
            P(GY, None),
            P(GX),
            P(GY),
            P(),
        ),
        out_specs=(P(None, GX, GY), P(None, GX, GY), P(None, GX, GY)),
        check_vma=False,
    )
```

```python
import functools

import jax
import jax.numpy as jnp
from jax import lax
from jax.experimental import pallas as pl
from jax.experimental.pallas import tpu as pltpu
from jax.sharding import Mesh
from jax.sharding import PartitionSpec as P

SUB = (("y", 8), ("xl", 2), ("c", 2), ("xh", 2), ("zh", 4), ("zl", 3))
GX = ("y", "xl", "c")
GY = ("xh", "zh", "zl")
QUAD = ("xl", "c")
BF = jnp.bfloat16
F32 = jnp.float32


def exchange(parts, axes):
    return lax.all_to_all(parts, axes, 0, 0)


def edges(block, axes, dim, count, periodic):
    forward = [(i, i + 1) for i in range(count - 1)]
    if periodic:
        forward.append((count - 1, 0))
    backward = [(target, source) for source, target in forward]
    low = lax.ppermute(lax.slice_in_dim(block, block.shape[dim] - 1, None, axis=dim), axes, forward)
    high = lax.ppermute(lax.slice_in_dim(block, 0, 1, axis=dim), axes, backward)
    return low, high


def centre_x(field):
    low, high = edges(field.astype(BF), GX, 1, 32, True)
    padded = jnp.concatenate([low.astype(F32), field, high.astype(F32)], axis=1)
    return 0.5 * (padded[:, 2:, :] - padded[:, :-2, :])


def centre_y(field):
    low, high = edges(field.astype(BF), GY, 2, 24, False)
    padded = jnp.concatenate([low.astype(F32), field, high.astype(F32)], axis=2)
    return 0.5 * (padded[:, :, 2:] - padded[:, :, :-2])


def call(kernel, out_shape, operands, scratch=(), flops=0):
    smem, vmem = pl.BlockSpec(memory_space=pltpu.SMEM), pl.BlockSpec(memory_space=pltpu.VMEM)
    outs = out_shape if isinstance(out_shape, list) else [out_shape]
    moved = sum(x.size * x.dtype.itemsize for x in list(operands[1:]) + outs)
    return pl.pallas_call(
        kernel,
        out_shape=out_shape,
        in_specs=[smem] + [vmem] * (len(operands) - 1),
        out_specs=[vmem] * len(outs) if isinstance(out_shape, list) else vmem,
        scratch_shapes=list(scratch),
        cost_estimate=pl.CostEstimate(flops=flops, bytes_accessed=moved, transcendentals=0),
        compiler_params=pltpu.CompilerParams(vmem_limit_bytes=12 << 20),
    )(*operands)


def window(place, half):
    return 9 * (place // 2) + 4 * (place % 2) + half


def quad_cut_kernel(me_ref, rows_ref, *out_refs):
    me = me_ref[0]
    for step, out_ref in enumerate(out_refs):
        other = lax.bitwise_xor(me, step)
        for y in range(8):
            start = pl.multiple_of((window(y, 0) + other) * 128, 128)
            back = lax.rem(256 - 64 * (y % 2) - 16 * other, 256)
            packed = pltpu.roll(rows_ref[:, pl.ds(start, 256)].astype(F32), back, 1)
            out_ref[:, 144 * y : 144 * (y + 1)] = packed[:, :144].astype(BF)


def quad_cut(me, rows):
    return call(quad_cut_kernel, [jax.ShapeDtypeStruct((144, 1152), BF)] * 4, (me, rows))


def quad_send(piece, step):
    return lax.ppermute(piece, QUAD, [(i, i ^ step) for i in range(4)])


def ring_cut_kernel(me_ref, first_ref, second_ref, *out_refs):
    me = me_ref[0]
    for step, out_ref in enumerate(out_refs):
        other = lax.rem(me + step, 3)
        for g in range(8):
            start = pl.multiple_of((3 * g + other) * 128, 128)
            out_ref[:128, g * 128 : (g + 1) * 128] = first_ref[:, pl.ds(start, 128)]
            out_ref[128:, g * 128 : (g + 1) * 128] = second_ref[:, pl.ds(start, 128)]


def ring_cut(me, first, second):
    return call(ring_cut_kernel, [jax.ShapeDtypeStruct((256, 1024), BF)] * 3, (me, first, second))


def ring_send(piece, step):
    return lax.ppermute(piece, "zl", [(i, (i + step) % 3) for i in range(3)])


def x_kernel(me_ref, held_ref, t0, t1, t2, t3, out_ref):
    me = me_ref[0]
    for step, table in enumerate((t0, t1, t2, t3)):
        part = jnp.dot(table[...], held_ref[...], preferred_element_type=F32)
        out_ref[lax.bitwise_xor(me, step)] = part.astype(BF)


def x_products(me, held, table):
    held = held.reshape(1152, 256)
    out = jax.ShapeDtypeStruct((4, 144, 256), BF)
    return call(x_kernel, out, (me, held, *table), flops=2 * 576 * 1152 * 256)


def y_kernel(offset, me_ref, held_ref, t0, t1, t2, out_ref, placed):
    me = me_ref[0]
    for g in range(8):
        placed[:, g * 128 : (g + 1) * 128] = held_ref[g]
    for step, table in enumerate((t0, t1, t2)):
        part = lax.dot_general(
            placed[...],
            table[offset : offset + 128, :],
            (((1,), (1,)), ((), ())),
            preferred_element_type=F32,
        )
        out_ref[lax.rem(me + 3 - step, 3)] = part.astype(BF)


def y_products(me, held, table):
    out = jax.ShapeDtypeStruct((3, 288, 128), BF)
    scratch = [pltpu.VMEM((288, 1024), BF)]
    return call(functools.partial(y_kernel, 0), out, (me, held, *table), scratch, flops=2 * 288 * 1024 * 384)


def added(got_ref):
    total = got_ref[0].astype(F32)
    for source in range(1, got_ref.shape[0]):
        total = total + got_ref[source].astype(F32)
    return total


def to_y_kernel(me_ref, got_ref, out_ref):
    total = added(got_ref).astype(BF)
    for g in range(8):
        out_ref[g, :144, :] = total[:, :128]
        out_ref[g, 144:, :] = total[:, 128:]


def scale_kernel(shift_ref, got_ref, x_ref, y_ref, out_ref):
    total = added(got_ref)
    denom = x_ref[...] + y_ref[...]
    for mode in range(2):
        rows = slice(144 * mode, 144 * (mode + 1))
        scaled = (total[rows] / (denom + shift_ref[mode])).astype(BF)
        for g in range(8):
            out_ref[g, rows, :] = scaled


def to_x_kernel(me_ref, got_ref, out_ref):
    total = added(got_ref)
    main = total[:288].astype(BF)
    sides = jnp.concatenate(
        [
            jnp.concatenate([total[288:296], total[304:312]], axis=0),
            jnp.concatenate([total[296:304], total[312:320]], axis=0),
        ],
        axis=1,
    ).astype(BF)
    for g in range(8):
        out_ref[g, :144, :128] = main[:144]
        out_ref[g, :144, 128:] = main[144:]
        out_ref[g, 144:, :] = sides


def nt_dot(left, right):
    return lax.dot_general(left, right, (((1,), (1,)), ((), ())), preferred_element_type=F32)


def x_back_kernel(me_ref, held_ref, t0, t1, t2, t3, lo_ref, hi_ref, out_ref, placed, side, last, first, sums):
    me = me_ref[0]
    sums[...] = jnp.zeros_like(sums)
    for y in range(8):
        placed[144 * y : 144 * (y + 1), :] = held_ref[y, :144, :]
        side[:, 144 * y : 144 * (y + 1)] = held_ref[y, 144:160, :144]
    last[0] = jnp.dot(lo_ref[...], placed[...], preferred_element_type=F32)[8:16]
    first[5] = jnp.dot(hi_ref[...], placed[...], preferred_element_type=F32)[:8]
    for step, table in enumerate((t0, t1, t2, t3)):
        target = lax.bitwise_xor(me, step)
        part = jnp.dot(table[...], placed[...], preferred_element_type=F32)
        out_ref[target, :144, :] = part.astype(BF)
        last[target + 1] = part[136:144]
        first[target + 1] = part[:8]
        sums[target, :, :144] = nt_dot(side[...], table[...])
    row = lax.broadcasted_iota(jnp.int32, (16, 256), 0)
    for target in range(4):
        low = jnp.broadcast_to(last[target][7:8], (16, 256))
        high = jnp.broadcast_to(first[target + 2][:1], (16, 256))
        group = jnp.where(row == 2, low, jnp.where(row == 3, high, sums[target]))
        out_ref[target, 144:160, :] = group.astype(BF)


def x_back_products(me, held, table, outer):
    scratch = [
        pltpu.VMEM((1152, 256), BF),
        pltpu.VMEM((16, 1152), BF),
        pltpu.VMEM((5, 8, 256), F32),
        pltpu.VMEM((6, 8, 256), F32),
        pltpu.VMEM((4, 16, 256), F32),
    ]
    out = jax.ShapeDtypeStruct((4, 160, 256), BF)
    return call(x_back_kernel, out, (me, held, *table, *outer), scratch, flops=2 * 576 * 1152 * 256)


def y_back_kernel(me_ref, held_ref, t0, t1, t2, lo_ref, hi_ref, out_ref, placed, last, first):
    me = me_ref[0]
    placed[288:, :] = jnp.zeros((112, 1024), BF)
    for g in range(8):
        placed[:288, g * 128 : (g + 1) * 128] = held_ref[g]
    last[0] = lo_ref[...]
    first[4] = hi_ref[...]
    for step, table in enumerate((t0, t1, t2)):
        target = lax.rem(me + 3 - step, 3)
        out_ref[target, :288, :] = nt_dot(placed[:288, :], table[128:, :]).astype(BF)
        last[target + 1] = table[240:256, :]
        first[target + 1] = table[128:144, :]
    row = lax.broadcasted_iota(jnp.int32, (16, 128), 0)
    lane = lax.broadcasted_iota(jnp.int32, (32, 128), 1)
    for target in range(3):
        rows = jnp.concatenate([last[target], first[target + 2]], axis=0)
        for mode in range(2):
            head = nt_dot(rows, placed[144 * mode : 144 * mode + 128, :])
            rest = nt_dot(rows, placed[144 * mode + 128 : 144 * mode + 256, :])
            rest = jnp.where(lane < 16, rest, 0.0)
            group = jnp.zeros((16, 128), F32)
            for at, value in ((0, head[15:16]), (1, head[16:17]), (8, rest[15:16]), (9, rest[16:17])):
                group = jnp.where(row == at, jnp.broadcast_to(value, (16, 128)), group)
            out_ref[target, 288 + 16 * mode : 304 + 16 * mode, :] = group.astype(BF)


def y_back_products(me, held, table, outer):
    scratch = [
        pltpu.VMEM((400, 1024), BF),
        pltpu.VMEM((4, 16, 1024), BF),
        pltpu.VMEM((5, 16, 1024), BF),
    ]
    out = jax.ShapeDtypeStruct((3, 320, 128), BF)
    return call(y_back_kernel, out, (me, held, *table, *outer), scratch, flops=2 * 288 * 1024 * 384)


def ring_outer(me, table):
    low = lax.dynamic_index_in_dim(jnp.stack([t[240:256] for t in table]), (me + 1) % 3, 0, False)
    high = lax.dynamic_index_in_dim(jnp.stack([t[128:144] for t in table]), me, 0, False)
    up = [(i, i + 1) for i in range(7)]
    down = [(i + 1, i) for i in range(7)]
    return lax.ppermute(low, ("xh", "zh"), up), lax.ppermute(high, ("xh", "zh"), down)


def quad_outer(me, table):
    low = lax.dynamic_index_in_dim(jnp.stack([t[128:144] for t in table]), me ^ 3, 0, False)
    high = lax.dynamic_index_in_dim(jnp.stack([t[:16] for t in table]), me, 0, False)
    up = [(i, (i + 1) % 8) for i in range(8)]
    down = [((i + 1) % 8, i) for i in range(8)]
    return lax.ppermute(low, "y", up), lax.ppermute(high, "y", down)


def to_x(block):
    return jnp.concatenate([block[:144], block[144:]], axis=1)


def to_y(block):
    return jnp.concatenate([block[:, :128], block[:, 128:]], axis=0)


def body(
    u_flow,
    v_flow,
    sea_mask,
    bottom_level,
    mode_project,
    mode_shape,
    forward_x,
    forward_y,
    inverse_x,
    inverse_y,
    eigen_x,
    eigen_y,
    mode_shift,
):
    level_ids = lax.broadcasted_iota(jnp.int32, u_flow.shape, 0)
    wet_int = sea_mask[None] * (level_ids < bottom_level[None]).astype(jnp.int32)
    wet = wet_int.astype(BF)
    flux_u = jnp.einsum("lm,lij->mij", mode_project, u_flow * wet, preferred_element_type=F32)
    flux_v = jnp.einsum("lm,lij->mij", mode_project, v_flow * wet, preferred_element_type=F32)
    flux_u = flux_u.astype(BF).astype(F32)
    flux_v = flux_v.astype(BF).astype(F32)
    mask_f = sea_mask.astype(F32)
    divergence = (mask_f[None] * (centre_x(flux_u) + centre_y(flux_v))).astype(BF)
    quad_me = (lax.axis_index("xl") * 2 + lax.axis_index("c")).astype(jnp.int32).reshape(1)
    ring_me = lax.axis_index("zl").astype(jnp.int32).reshape(1)
    cut_fx, cut_y = quad_cut(quad_me, forward_x), ring_cut(ring_me, forward_y, inverse_y)
    divergence, y_one, fx_two = lax.optimization_barrier((divergence, ring_send(cut_y[1], 1), cut_fx[2]))
    cut_fx = [cut_fx[0], cut_fx[1], fx_two, cut_fx[3]]
    table_fx = [cut_fx[0]] + [quad_send(cut_fx[step], step) for step in (1, 2, 3)]
    y_two = ring_send(cut_y[2], 2)
    block = to_x(divergence.reshape(288, 128))
    held = exchange(jnp.broadcast_to(block[None], (8, 144, 256)), "y")
    got = exchange(x_products(quad_me, held, table_fx), QUAD)
    got, y_two = lax.optimization_barrier((got, y_two))
    cut_ix = quad_cut(quad_me, inverse_x)
    table_y = (cut_y[0], y_one, y_two)
    spread = jax.ShapeDtypeStruct((8, 288, 128), BF)
    held = exchange(call(to_y_kernel, spread, (quad_me, got)), ("xh", "zh"))
    held, table_ix = lax.optimization_barrier(
        (held, [cut_ix[0]] + [quad_send(cut_ix[step], step) for step in (1, 2, 3)])
    )
    got = exchange(y_products(ring_me, held, table_y), "zl")
    eigen = (eigen_x.reshape(144, 1), eigen_y.reshape(1, 128))
    held = exchange(call(scale_kernel, spread, (mode_shift, got, *eigen)), ("xh", "zh"))
    outer_y, outer_x = ring_outer(ring_me[0], table_y), quad_outer(quad_me[0], table_ix)
    held, outer_x = lax.optimization_barrier((held, outer_x))
    got = exchange(y_back_products(ring_me, held, table_y, outer_y), "zl")
    spread = jax.ShapeDtypeStruct((8, 160, 256), BF)
    held = exchange(call(to_x_kernel, spread, (quad_me, got)), "y")
    parts = exchange(x_back_products(quad_me, held, table_ix, outer_x), QUAD)
    total = jnp.sum(parts.astype(F32), axis=0)
    pressure = to_y(total[:144]).reshape(2, 144, 128)
    low, high = total[146].reshape(2, 1, 128), total[147].reshape(2, 1, 128)
    padded = jnp.concatenate([low, pressure, high], axis=1)
    grad_x = 0.5 * (padded[:, 2:, :] - padded[:, :-2, :])
    sides = jnp.stack([total[144:146, :144], total[152:154, :144]])
    padded = jnp.concatenate([sides[:, 0, :, None], pressure, sides[:, 1, :, None]], axis=2)
    grad_y = 0.5 * (padded[:, :, 2:] - padded[:, :, :-2])
    wet_f = wet_int.astype(F32)
    shape_zero = mode_shape[:, 0][:, None, None]
    shape_one = mode_shape[:, 1][:, None, None]
    u_correct = (-wet_f * (shape_zero * grad_x[0][None] + shape_one * grad_x[1][None])).astype(BF)
    v_correct = (-wet_f * (shape_zero * grad_y[0][None] + shape_one * grad_y[1][None])).astype(BF)
    return (u_correct, v_correct, pressure)


def solution(mesh):
    sub = Mesh(mesh.devices.reshape([n for _, n in SUB]), [name for name, _ in SUB])
    return jax.shard_map(
        body,
        mesh=sub,
        in_specs=(
            P(None, GX, GY),
            P(None, GX, GY),
            P(GX, GY),
            P(GX, GY),
            P(),
            P(),
            P(GX, None),
            P(GY, None),
            P(GX, None),
            P(GY, None),
            P(GX),
            P(GY),
            P(),
        ),
        out_specs=(P(None, GX, GY), P(None, GX, GY), P(None, GX, GY)),
        check_vma=False,
    )
```

```python
import functools

import jax
import jax.numpy as jnp
from jax import lax
from jax.experimental import pallas as pl
from jax.experimental.pallas import tpu as pltpu
from jax.sharding import Mesh
from jax.sharding import PartitionSpec as P

SUB = (("y", 8), ("xl", 2), ("c", 2), ("xh", 2), ("zh", 4), ("zl", 3))
GX = ("y", "xl", "c")
GY = ("xh", "zh", "zl")
QUAD = ("xl", "c")
BF = jnp.bfloat16
F32 = jnp.float32


def exchange(parts, axes):
    return lax.all_to_all(parts, axes, 0, 0)


def edges(block, axes, dim, count, periodic):
    forward = [(i, i + 1) for i in range(count - 1)]
    if periodic:
        forward.append((count - 1, 0))
    backward = [(target, source) for source, target in forward]
    low = lax.ppermute(lax.slice_in_dim(block, block.shape[dim] - 1, None, axis=dim), axes, forward)
    high = lax.ppermute(lax.slice_in_dim(block, 0, 1, axis=dim), axes, backward)
    return low, high


def centre_x(field):
    low, high = edges(field.astype(BF), GX, 1, 32, True)
    padded = jnp.concatenate([low.astype(F32), field, high.astype(F32)], axis=1)
    return 0.5 * (padded[:, 2:, :] - padded[:, :-2, :])


def centre_y(field):
    low, high = edges(field.astype(BF), GY, 2, 24, False)
    padded = jnp.concatenate([low.astype(F32), field, high.astype(F32)], axis=2)
    return 0.5 * (padded[:, :, 2:] - padded[:, :, :-2])


def call(kernel, out_shape, operands, scratch=(), flops=0):
    smem, vmem = pl.BlockSpec(memory_space=pltpu.SMEM), pl.BlockSpec(memory_space=pltpu.VMEM)
    outs = out_shape if isinstance(out_shape, list) else [out_shape]
    moved = sum(x.size * x.dtype.itemsize for x in list(operands[1:]) + outs)
    return pl.pallas_call(
        kernel,
        out_shape=out_shape,
        in_specs=[smem] + [vmem] * (len(operands) - 1),
        out_specs=[vmem] * len(outs) if isinstance(out_shape, list) else vmem,
        scratch_shapes=list(scratch),
        cost_estimate=pl.CostEstimate(flops=flops, bytes_accessed=moved, transcendentals=0),
        compiler_params=pltpu.CompilerParams(vmem_limit_bytes=12 << 20),
    )(*operands)


def window(place, half):
    return 9 * (place // 2) + 4 * (place % 2) + half


def quad_cut_kernel(me_ref, rows_ref, *out_refs):
    me = me_ref[0]
    for step, out_ref in enumerate(out_refs):
        other = lax.bitwise_xor(me, step)
        for y in range(8):
            start = pl.multiple_of((window(y, 0) + other) * 128, 128)
            back = lax.rem(256 - 64 * (y % 2) - 16 * other, 256)
            packed = pltpu.roll(rows_ref[:, pl.ds(start, 256)].astype(F32), back, 1)
            out_ref[:, 144 * y : 144 * (y + 1)] = packed[:, :144].astype(BF)


def quad_cut(me, rows):
    return call(quad_cut_kernel, [jax.ShapeDtypeStruct((144, 1152), BF)] * 4, (me, rows))


def quad_send(piece, step):
    return lax.ppermute(piece, QUAD, [(i, i ^ step) for i in range(4)])


def ring_cut_kernel(me_ref, first_ref, second_ref, *out_refs):
    me = me_ref[0]
    for step, out_ref in enumerate(out_refs):
        other = lax.rem(me + step, 3)
        for g in range(8):
            start = pl.multiple_of((3 * g + other) * 128, 128)
            out_ref[:128, g * 128 : (g + 1) * 128] = first_ref[:, pl.ds(start, 128)]
            out_ref[128:, g * 128 : (g + 1) * 128] = second_ref[:, pl.ds(start, 128)]


def ring_cut(me, first, second):
    return call(ring_cut_kernel, [jax.ShapeDtypeStruct((256, 1024), BF)] * 3, (me, first, second))


def ring_send(piece, step):
    return lax.ppermute(piece, "zl", [(i, (i + step) % 3) for i in range(3)])


def x_kernel(me_ref, held_ref, t0, t1, t2, t3, out_ref):
    me = me_ref[0]
    for step, table in enumerate((t0, t1, t2, t3)):
        part = jnp.dot(table[...], held_ref[...], preferred_element_type=F32)
        out_ref[lax.bitwise_xor(me, step)] = part.astype(BF)


def x_products(me, held, table):
    held = held.reshape(1152, 256)
    out = jax.ShapeDtypeStruct((4, 144, 256), BF)
    return call(x_kernel, out, (me, held, *table), flops=2 * 576 * 1152 * 256)


def y_kernel(offset, me_ref, held_ref, t0, t1, t2, out_ref, placed):
    me = me_ref[0]
    for g in range(8):
        placed[:, g * 128 : (g + 1) * 128] = held_ref[g]
    for step, table in enumerate((t0, t1, t2)):
        part = lax.dot_general(
            placed[...],
            table[offset : offset + 128, :],
            (((1,), (1,)), ((), ())),
            preferred_element_type=F32,
        )
        out_ref[lax.rem(me + 3 - step, 3)] = part.astype(BF)


def y_products(me, held, table):
    out = jax.ShapeDtypeStruct((3, 288, 128), BF)
    scratch = [pltpu.VMEM((288, 1024), BF)]
    return call(functools.partial(y_kernel, 0), out, (me, held, *table), scratch, flops=2 * 288 * 1024 * 384)


def added(got_ref):
    total = got_ref[0].astype(F32)
    for source in range(1, got_ref.shape[0]):
        total = total + got_ref[source].astype(F32)
    return total


def to_y_kernel(me_ref, got_ref, out_ref):
    total = added(got_ref).astype(BF)
    for g in range(8):
        out_ref[g, :144, :] = total[:, :128]
        out_ref[g, 144:, :] = total[:, 128:]


def scale_kernel(shift_ref, got_ref, denom_ref, out_ref):
    total = added(got_ref)
    denom = denom_ref[...]
    for mode in range(2):
        rows = slice(144 * mode, 144 * (mode + 1))
        scaled = (total[rows] / (denom + shift_ref[mode])).astype(BF)
        for g in range(8):
            out_ref[g, rows, :] = scaled


def to_x_kernel(me_ref, got_ref, out_ref):
    total = added(got_ref)
    main = total[:288].astype(BF)
    sides = jnp.concatenate(
        [
            jnp.concatenate([total[288:296], total[304:312]], axis=0),
            jnp.concatenate([total[296:304], total[312:320]], axis=0),
        ],
        axis=1,
    ).astype(BF)
    for g in range(8):
        out_ref[g, :144, :128] = main[:144]
        out_ref[g, :144, 128:] = main[144:]
        out_ref[g, 144:, :] = sides


def nt_dot(left, right):
    return lax.dot_general(left, right, (((1,), (1,)), ((), ())), preferred_element_type=F32)


def x_back_kernel(me_ref, held_ref, t0, t1, t2, t3, lo_ref, hi_ref, out_ref, placed, side, last, first, sums):
    me = me_ref[0]
    sums[...] = jnp.zeros_like(sums)
    for y in range(8):
        placed[144 * y : 144 * (y + 1), :] = held_ref[y, :144, :]
        side[:, 144 * y : 144 * (y + 1)] = held_ref[y, 144:160, :144]
    last[0] = jnp.dot(lo_ref[...], placed[...], preferred_element_type=F32)[8:16]
    first[5] = jnp.dot(hi_ref[...], placed[...], preferred_element_type=F32)[:8]
    for step, table in enumerate((t0, t1, t2, t3)):
        target = lax.bitwise_xor(me, step)
        part = jnp.dot(table[...], placed[...], preferred_element_type=F32)
        out_ref[target, :144, :] = part.astype(BF)
        last[target + 1] = part[136:144]
        first[target + 1] = part[:8]
        sums[target, :, :144] = nt_dot(side[...], table[...])
    row = lax.broadcasted_iota(jnp.int32, (16, 256), 0)
    for target in range(4):
        low = jnp.broadcast_to(last[target][7:8], (16, 256))
        high = jnp.broadcast_to(first[target + 2][:1], (16, 256))
        group = jnp.where(row == 2, low, jnp.where(row == 3, high, sums[target]))
        out_ref[target, 144:160, :] = group.astype(BF)


def x_back_products(me, held, table, outer):
    scratch = [
        pltpu.VMEM((1152, 256), BF),
        pltpu.VMEM((16, 1152), BF),
        pltpu.VMEM((5, 8, 256), F32),
        pltpu.VMEM((6, 8, 256), F32),
        pltpu.VMEM((4, 16, 256), F32),
    ]
    out = jax.ShapeDtypeStruct((4, 160, 256), BF)
    return call(x_back_kernel, out, (me, held, *table, *outer), scratch, flops=2 * 576 * 1152 * 256)


def y_back_kernel(me_ref, held_ref, t0, t1, t2, lo_ref, hi_ref, out_ref, placed, last, first):
    me = me_ref[0]
    placed[288:, :] = jnp.zeros((112, 1024), BF)
    for g in range(8):
        placed[:288, g * 128 : (g + 1) * 128] = held_ref[g]
    last[0] = lo_ref[...]
    first[4] = hi_ref[...]
    for step, table in enumerate((t0, t1, t2)):
        target = lax.rem(me + 3 - step, 3)
        out_ref[target, :288, :] = nt_dot(placed[:288, :], table[128:, :]).astype(BF)
        last[target + 1] = table[240:256, :]
        first[target + 1] = table[128:144, :]
    row = lax.broadcasted_iota(jnp.int32, (16, 128), 0)
    lane = lax.broadcasted_iota(jnp.int32, (32, 128), 1)
    for target in range(3):
        rows = jnp.concatenate([last[target], first[target + 2]], axis=0)
        for mode in range(2):
            head = nt_dot(rows, placed[144 * mode : 144 * mode + 128, :])
            rest = nt_dot(rows, placed[144 * mode + 128 : 144 * mode + 256, :])
            rest = jnp.where(lane < 16, rest, 0.0)
            group = jnp.zeros((16, 128), F32)
            for at, value in ((0, head[15:16]), (1, head[16:17]), (8, rest[15:16]), (9, rest[16:17])):
                group = jnp.where(row == at, jnp.broadcast_to(value, (16, 128)), group)
            out_ref[target, 288 + 16 * mode : 304 + 16 * mode, :] = group.astype(BF)


def y_back_products(me, held, table, outer):
    scratch = [
        pltpu.VMEM((400, 1024), BF),
        pltpu.VMEM((4, 16, 1024), BF),
        pltpu.VMEM((5, 16, 1024), BF),
    ]
    out = jax.ShapeDtypeStruct((3, 320, 128), BF)
    return call(y_back_kernel, out, (me, held, *table, *outer), scratch, flops=2 * 288 * 1024 * 384)


def ring_outer(me, table):
    low = lax.dynamic_index_in_dim(jnp.stack([t[240:256] for t in table]), (me + 1) % 3, 0, False)
    high = lax.dynamic_index_in_dim(jnp.stack([t[128:144] for t in table]), me, 0, False)
    up = [(i, i + 1) for i in range(7)]
    down = [(i + 1, i) for i in range(7)]
    return lax.ppermute(low, ("xh", "zh"), up), lax.ppermute(high, ("xh", "zh"), down)


def quad_outer(me, table):
    low = lax.dynamic_index_in_dim(jnp.stack([t[128:144] for t in table]), me ^ 3, 0, False)
    high = lax.dynamic_index_in_dim(jnp.stack([t[:16] for t in table]), me, 0, False)
    up = [(i, (i + 1) % 8) for i in range(8)]
    down = [((i + 1) % 8, i) for i in range(8)]
    return lax.ppermute(low, "y", up), lax.ppermute(high, "y", down)


def to_x(block):
    return jnp.concatenate([block[:144], block[144:]], axis=1)


def to_y(block):
    return jnp.concatenate([block[:, :128], block[:, 128:]], axis=0)


def body(
    u_flow,
    v_flow,
    sea_mask,
    bottom_level,
    mode_project,
    mode_shape,
    forward_x,
    forward_y,
    inverse_x,
    inverse_y,
    eigen_x,
    eigen_y,
    mode_shift,
):
    level_ids = lax.broadcasted_iota(jnp.int32, u_flow.shape, 0)
    wet_int = sea_mask[None] * (level_ids < bottom_level[None]).astype(jnp.int32)
    wet = wet_int.astype(BF)
    flux_u = jnp.einsum("lm,lij->mij", mode_project, u_flow * wet, preferred_element_type=F32)
    flux_v = jnp.einsum("lm,lij->mij", mode_project, v_flow * wet, preferred_element_type=F32)
    flux_u = flux_u.astype(BF).astype(F32)
    flux_v = flux_v.astype(BF).astype(F32)
    mask_f = sea_mask.astype(F32)
    divergence = (mask_f[None] * (centre_x(flux_u) + centre_y(flux_v))).astype(BF)
    quad_me = (lax.axis_index("xl") * 2 + lax.axis_index("c")).astype(jnp.int32).reshape(1)
    ring_me = lax.axis_index("zl").astype(jnp.int32).reshape(1)
    cut_fx, cut_y = quad_cut(quad_me, forward_x), ring_cut(ring_me, forward_y, inverse_y)
    divergence, y_one, fx_two = lax.optimization_barrier((divergence, ring_send(cut_y[1], 1), cut_fx[2]))
    cut_fx = [cut_fx[0], cut_fx[1], fx_two, cut_fx[3]]
    table_fx = [cut_fx[0]] + [quad_send(cut_fx[step], step) for step in (1, 2, 3)]
    y_two = ring_send(cut_y[2], 2)
    block = to_x(divergence.reshape(288, 128))
    held = exchange(jnp.broadcast_to(block[None], (8, 144, 256)), "y")
    got = exchange(x_products(quad_me, held, table_fx), QUAD)
    shapes = (mode_shape[:, 0], mode_shape[:, 1])
    got, y_two, (shape_zero, shape_one) = lax.optimization_barrier((got, y_two, shapes))
    cut_ix = quad_cut(quad_me, inverse_x)
    table_y = (cut_y[0], y_one, y_two)
    spread = jax.ShapeDtypeStruct((8, 288, 128), BF)
    held = exchange(call(to_y_kernel, spread, (quad_me, got)), ("xh", "zh"))
    table_ix = [cut_ix[0]] + [quad_send(cut_ix[step], step) for step in (1, 2, 3)]
    denom = eigen_x[:, None] + eigen_y[None, :]
    held, table_ix, denom = lax.optimization_barrier((held, table_ix, denom))
    got = exchange(y_products(ring_me, held, table_y), "zl")
    got, table_ix, table_y = lax.optimization_barrier((got, table_ix, table_y))
    outer_y = ring_outer(ring_me[0], table_y)
    held = exchange(call(scale_kernel, spread, (mode_shift, got, denom)), ("xh", "zh"))
    outer_x = quad_outer(quad_me[0], table_ix)
    held, outer_x = lax.optimization_barrier((held, outer_x))
    got = exchange(y_back_products(ring_me, held, table_y, outer_y), "zl")
    spread = jax.ShapeDtypeStruct((8, 160, 256), BF)
    held = exchange(call(to_x_kernel, spread, (quad_me, got)), "y")
    parts = exchange(x_back_products(quad_me, held, table_ix, outer_x), QUAD)
    total = jnp.sum(parts.astype(F32), axis=0)
    pressure = to_y(total[:144]).reshape(2, 144, 128)
    low, high = total[146].reshape(2, 1, 128), total[147].reshape(2, 1, 128)
    padded = jnp.concatenate([low, pressure, high], axis=1)
    grad_x = 0.5 * (padded[:, 2:, :] - padded[:, :-2, :])
    sides = jnp.stack([total[144:146, :144], total[152:154, :144]])
    padded = jnp.concatenate([sides[:, 0, :, None], pressure, sides[:, 1, :, None]], axis=2)
    grad_y = 0.5 * (padded[:, :, 2:] - padded[:, :, :-2])
    wet_f = wet_int.astype(F32)
    shape_zero = shape_zero[:, None, None]
    shape_one = shape_one[:, None, None]
    u_correct = (-wet_f * (shape_zero * grad_x[0][None] + shape_one * grad_x[1][None])).astype(BF)
    v_correct = (-wet_f * (shape_zero * grad_y[0][None] + shape_one * grad_y[1][None])).astype(BF)
    return (u_correct, v_correct, pressure)


def solution(mesh):
    sub = Mesh(mesh.devices.reshape([n for _, n in SUB]), [name for name, _ in SUB])
    return jax.shard_map(
        body,
        mesh=sub,
        in_specs=(
            P(None, GX, GY),
            P(None, GX, GY),
            P(GX, GY),
            P(GX, GY),
            P(),
            P(),
            P(GX, None),
            P(GY, None),
            P(GX, None),
            P(GY, None),
            P(GX),
            P(GY),
            P(),
        ),
        out_specs=(P(None, GX, GY), P(None, GX, GY), P(None, GX, GY)),
        check_vma=False,
    )
```

```python
import functools

import jax
import jax.numpy as jnp
from jax import lax
from jax.experimental import pallas as pl
from jax.experimental.pallas import tpu as pltpu
from jax.sharding import Mesh
from jax.sharding import PartitionSpec as P

SUB = (("y", 8), ("xl", 2), ("c", 2), ("xh", 2), ("zh", 4), ("zl", 3))
GX = ("y", "xl", "c")
GY = ("xh", "zh", "zl")
QUAD = ("xl", "c")
BF = jnp.bfloat16
F32 = jnp.float32


def exchange(parts, axes):
    return lax.all_to_all(parts, axes, 0, 0)


def edges(block, axes, dim, count, periodic):
    forward = [(i, i + 1) for i in range(count - 1)]
    if periodic:
        forward.append((count - 1, 0))
    backward = [(target, source) for source, target in forward]
    low = lax.ppermute(lax.slice_in_dim(block, block.shape[dim] - 1, None, axis=dim), axes, forward)
    high = lax.ppermute(lax.slice_in_dim(block, 0, 1, axis=dim), axes, backward)
    return low, high


def centre_x(field):
    low, high = edges(field.astype(BF), GX, 1, 32, True)
    padded = jnp.concatenate([low.astype(F32), field, high.astype(F32)], axis=1)
    return 0.5 * (padded[:, 2:, :] - padded[:, :-2, :])


def centre_y(field):
    low, high = edges(field.astype(BF), GY, 2, 24, False)
    padded = jnp.concatenate([low.astype(F32), field, high.astype(F32)], axis=2)
    return 0.5 * (padded[:, :, 2:] - padded[:, :, :-2])


def call(kernel, out_shape, operands, scratch=(), flops=0):
    smem, vmem = pl.BlockSpec(memory_space=pltpu.SMEM), pl.BlockSpec(memory_space=pltpu.VMEM)
    outs = out_shape if isinstance(out_shape, list) else [out_shape]
    moved = sum(x.size * x.dtype.itemsize for x in list(operands[1:]) + outs)
    return pl.pallas_call(
        kernel,
        out_shape=out_shape,
        in_specs=[smem] + [vmem] * (len(operands) - 1),
        out_specs=[vmem] * len(outs) if isinstance(out_shape, list) else vmem,
        scratch_shapes=list(scratch),
        cost_estimate=pl.CostEstimate(flops=flops, bytes_accessed=moved, transcendentals=0),
        compiler_params=pltpu.CompilerParams(vmem_limit_bytes=12 << 20),
    )(*operands)


def window(place, half):
    return 9 * (place // 2) + 4 * (place % 2) + half


def quad_cut_kernel(me_ref, rows_ref, *out_refs):
    me = me_ref[0]
    for step, out_ref in enumerate(out_refs):
        other = lax.bitwise_xor(me, step)
        for y in range(8):
            start = pl.multiple_of((window(y, 0) + other) * 128, 128)
            back = lax.rem(256 - 64 * (y % 2) - 16 * other, 256)
            packed = pltpu.roll(rows_ref[:, pl.ds(start, 256)].astype(F32), back, 1)
            out_ref[:, 144 * y : 144 * (y + 1)] = packed[:, :144].astype(BF)


def quad_cut(me, rows):
    return call(quad_cut_kernel, [jax.ShapeDtypeStruct((144, 1152), BF)] * 4, (me, rows))


def quad_send(piece, step):
    return lax.ppermute(piece, QUAD, [(i, i ^ step) for i in range(4)])


def ring_cut_kernel(me_ref, first_ref, second_ref, *out_refs):
    me = me_ref[0]
    for step, out_ref in enumerate(out_refs):
        other = lax.rem(me + step, 3)
        for g in range(8):
            start = pl.multiple_of((3 * g + other) * 128, 128)
            out_ref[:128, g * 128 : (g + 1) * 128] = first_ref[:, pl.ds(start, 128)]
            out_ref[128:, g * 128 : (g + 1) * 128] = second_ref[:, pl.ds(start, 128)]


def ring_cut(me, first, second):
    return call(ring_cut_kernel, [jax.ShapeDtypeStruct((256, 1024), BF)] * 3, (me, first, second))


def ring_send(piece, step):
    return lax.ppermute(piece, "zl", [(i, (i + step) % 3) for i in range(3)])


def x_kernel(me_ref, held_ref, t0, t1, t2, t3, out_ref):
    me = me_ref[0]
    for step, table in enumerate((t0, t1, t2, t3)):
        part = jnp.dot(table[...], held_ref[...], preferred_element_type=F32)
        out_ref[lax.bitwise_xor(me, step)] = part.astype(BF)


def x_products(me, held, table):
    held = held.reshape(1152, 256)
    out = jax.ShapeDtypeStruct((4, 144, 256), BF)
    return call(x_kernel, out, (me, held, *table), flops=2 * 576 * 1152 * 256)


def y_kernel(offset, me_ref, held_ref, t0, t1, t2, out_ref, placed):
    me = me_ref[0]
    for g in range(8):
        placed[:, g * 128 : (g + 1) * 128] = held_ref[g]
    for step, table in enumerate((t0, t1, t2)):
        part = lax.dot_general(
            placed[...],
            table[offset : offset + 128, :],
            (((1,), (1,)), ((), ())),
            preferred_element_type=F32,
        )
        out_ref[lax.rem(me + 3 - step, 3)] = part.astype(BF)


def y_products(me, held, table):
    out = jax.ShapeDtypeStruct((3, 288, 128), BF)
    scratch = [pltpu.VMEM((288, 1024), BF)]
    return call(functools.partial(y_kernel, 0), out, (me, held, *table), scratch, flops=2 * 288 * 1024 * 384)


def added(got_ref):
    total = got_ref[0].astype(F32)
    for source in range(1, got_ref.shape[0]):
        total = total + got_ref[source].astype(F32)
    return total


def to_y_kernel(me_ref, got_ref, out_ref):
    total = added(got_ref).astype(BF)
    for g in range(8):
        out_ref[g, :144, :] = total[:, :128]
        out_ref[g, 144:, :] = total[:, 128:]


def scale_kernel(shift_ref, got_ref, denom_ref, out_ref):
    total = added(got_ref)
    denom = denom_ref[...]
    for mode in range(2):
        rows = slice(144 * mode, 144 * (mode + 1))
        scaled = (total[rows] / (denom + shift_ref[mode])).astype(BF)
        for g in range(8):
            out_ref[g, rows, :] = scaled


def to_x_kernel(me_ref, got_ref, out_ref):
    total = added(got_ref)
    main = total[:288].astype(BF)
    sides = jnp.concatenate(
        [
            jnp.concatenate([total[288:296], total[304:312]], axis=0),
            jnp.concatenate([total[296:304], total[312:320]], axis=0),
        ],
        axis=1,
    ).astype(BF)
    for g in range(8):
        out_ref[g, :144, :128] = main[:144]
        out_ref[g, :144, 128:] = main[144:]
        out_ref[g, 144:, :] = sides


def nt_dot(left, right):
    return lax.dot_general(left, right, (((1,), (1,)), ((), ())), preferred_element_type=F32)


def x_back_kernel(me_ref, held_ref, t0, t1, t2, t3, lo_ref, hi_ref, out_ref, placed, side, last, first, sums):
    me = me_ref[0]
    sums[...] = jnp.zeros_like(sums)
    for y in range(8):
        placed[144 * y : 144 * (y + 1), :] = held_ref[y, :144, :]
        side[:, 144 * y : 144 * (y + 1)] = held_ref[y, 144:160, :144]
    last[0] = jnp.dot(lo_ref[...], placed[...], preferred_element_type=F32)[8:16]
    first[5] = jnp.dot(hi_ref[...], placed[...], preferred_element_type=F32)[:8]
    for step, table in enumerate((t0, t1, t2, t3)):
        target = lax.bitwise_xor(me, step)
        part = jnp.dot(table[...], placed[...], preferred_element_type=F32)
        out_ref[target, :144, :] = part.astype(BF)
        last[target + 1] = part[136:144]
        first[target + 1] = part[:8]
        sums[target, :, :144] = nt_dot(side[...], table[...])
    row = lax.broadcasted_iota(jnp.int32, (16, 256), 0)
    for target in range(4):
        low = jnp.broadcast_to(last[target][7:8], (16, 256))
        high = jnp.broadcast_to(first[target + 2][:1], (16, 256))
        group = jnp.where(row == 2, low, jnp.where(row == 3, high, sums[target]))
        out_ref[target, 144:160, :] = group.astype(BF)


def x_back_products(me, held, table, outer):
    scratch = [
        pltpu.VMEM((1152, 256), BF),
        pltpu.VMEM((16, 1152), BF),
        pltpu.VMEM((5, 8, 256), F32),
        pltpu.VMEM((6, 8, 256), F32),
        pltpu.VMEM((4, 16, 256), F32),
    ]
    out = jax.ShapeDtypeStruct((4, 160, 256), BF)
    return call(x_back_kernel, out, (me, held, *table, *outer), scratch, flops=2 * 576 * 1152 * 256)


def y_back_kernel(me_ref, held_ref, t0, t1, t2, lo_ref, hi_ref, out_ref, placed, last, first):
    me = me_ref[0]
    placed[288:, :] = jnp.zeros((112, 1024), BF)
    for g in range(8):
        placed[:288, g * 128 : (g + 1) * 128] = held_ref[g]
    last[0] = lo_ref[...]
    first[4] = hi_ref[...]
    for step, table in enumerate((t0, t1, t2)):
        target = lax.rem(me + 3 - step, 3)
        out_ref[target, :288, :] = nt_dot(placed[:288, :], table[128:, :]).astype(BF)
        last[target + 1] = table[240:256, :]
        first[target + 1] = table[128:144, :]
    row = lax.broadcasted_iota(jnp.int32, (16, 128), 0)
    lane = lax.broadcasted_iota(jnp.int32, (32, 128), 1)
    for target in range(3):
        rows = jnp.concatenate([last[target], first[target + 2]], axis=0)
        for mode in range(2):
            head = nt_dot(rows, placed[144 * mode : 144 * mode + 128, :])
            rest = nt_dot(rows, placed[144 * mode + 128 : 144 * mode + 256, :])
            rest = jnp.where(lane < 16, rest, 0.0)
            group = jnp.zeros((16, 128), F32)
            for at, value in ((0, head[15:16]), (1, head[16:17]), (8, rest[15:16]), (9, rest[16:17])):
                group = jnp.where(row == at, jnp.broadcast_to(value, (16, 128)), group)
            out_ref[target, 288 + 16 * mode : 304 + 16 * mode, :] = group.astype(BF)


def y_back_products(me, held, table, outer):
    scratch = [
        pltpu.VMEM((400, 1024), BF),
        pltpu.VMEM((4, 16, 1024), BF),
        pltpu.VMEM((5, 16, 1024), BF),
    ]
    out = jax.ShapeDtypeStruct((3, 320, 128), BF)
    return call(y_back_kernel, out, (me, held, *table, *outer), scratch, flops=2 * 288 * 1024 * 384)


def ring_outer(me, table):
    low = lax.dynamic_index_in_dim(jnp.stack([t[240:256] for t in table]), (me + 1) % 3, 0, False)
    high = lax.dynamic_index_in_dim(jnp.stack([t[128:144] for t in table]), me, 0, False)
    up = [(i, i + 1) for i in range(7)]
    down = [(i + 1, i) for i in range(7)]
    return lax.ppermute(low, ("xh", "zh"), up), lax.ppermute(high, ("xh", "zh"), down)


def quad_outer(me, table):
    low = lax.dynamic_index_in_dim(jnp.stack([t[128:144] for t in table]), me ^ 3, 0, False)
    high = lax.dynamic_index_in_dim(jnp.stack([t[:16] for t in table]), me, 0, False)
    up = [(i, (i + 1) % 8) for i in range(8)]
    down = [((i + 1) % 8, i) for i in range(8)]
    return lax.ppermute(low, "y", up), lax.ppermute(high, "y", down)


def to_x(block):
    return jnp.concatenate([block[:144], block[144:]], axis=1)


def to_y(block):
    return jnp.concatenate([block[:, :128], block[:, 128:]], axis=0)


def body(
    u_flow,
    v_flow,
    sea_mask,
    bottom_level,
    mode_project,
    mode_shape,
    forward_x,
    forward_y,
    inverse_x,
    inverse_y,
    eigen_x,
    eigen_y,
    mode_shift,
):
    level_ids = lax.broadcasted_iota(jnp.int32, u_flow.shape, 0)
    wet_int = sea_mask[None] * (level_ids < bottom_level[None]).astype(jnp.int32)
    wet = wet_int.astype(BF)
    flux_u = jnp.einsum("lm,lij->mij", mode_project, u_flow * wet, preferred_element_type=F32)
    flux_v = jnp.einsum("lm,lij->mij", mode_project, v_flow * wet, preferred_element_type=F32)
    flux_u = flux_u.astype(BF).astype(F32)
    flux_v = flux_v.astype(BF).astype(F32)
    mask_f = sea_mask.astype(F32)
    divergence = (mask_f[None] * (centre_x(flux_u) + centre_y(flux_v))).astype(BF)
    quad_me = (lax.axis_index("xl") * 2 + lax.axis_index("c")).astype(jnp.int32).reshape(1)
    ring_me = lax.axis_index("zl").astype(jnp.int32).reshape(1)
    cut_fx, cut_y = quad_cut(quad_me, forward_x), ring_cut(ring_me, forward_y, inverse_y)
    divergence, y_one, fx_two = lax.optimization_barrier((divergence, ring_send(cut_y[1], 1), cut_fx[2]))
    cut_fx = [cut_fx[0], cut_fx[1], fx_two, cut_fx[3]]
    fx_two, fx_three = quad_send(cut_fx[2], 2), quad_send(cut_fx[3], 3)
    core, fx_two = lax.optimization_barrier((cut_fx[1], fx_two))
    table_fx = (cut_fx[0], quad_send(core, 1), fx_two, fx_three)
    y_two = ring_send(cut_y[2], 2)
    block = to_x(divergence.reshape(288, 128))
    held = exchange(jnp.broadcast_to(block[None], (8, 144, 256)), "y")
    got = exchange(x_products(quad_me, held, table_fx), QUAD)
    shapes = (mode_shape[:, 0], mode_shape[:, 1])
    got, y_two, (shape_zero, shape_one) = lax.optimization_barrier((got, y_two, shapes))
    cut_ix = quad_cut(quad_me, inverse_x)
    table_y = (cut_y[0], y_one, y_two)
    spread = jax.ShapeDtypeStruct((8, 288, 128), BF)
    held = exchange(call(to_y_kernel, spread, (quad_me, got)), ("xh", "zh"))
    ix_two, ix_three = quad_send(cut_ix[2], 2), quad_send(cut_ix[3], 3)
    core, ix_two = lax.optimization_barrier((cut_ix[1], ix_two))
    table_ix = (cut_ix[0], quad_send(core, 1), ix_two, ix_three)
    denom = eigen_x[:, None] + eigen_y[None, :]
    held, table_ix, denom = lax.optimization_barrier((held, table_ix, denom))
    got = exchange(y_products(ring_me, held, table_y), "zl")
    got, table_ix, table_y = lax.optimization_barrier((got, table_ix, table_y))
    outer_y = ring_outer(ring_me[0], table_y)
    held = exchange(call(scale_kernel, spread, (mode_shift, got, denom)), ("xh", "zh"))
    outer_x = quad_outer(quad_me[0], table_ix)
    held, outer_x = lax.optimization_barrier((held, outer_x))
    got = exchange(y_back_products(ring_me, held, table_y, outer_y), "zl")
    spread = jax.ShapeDtypeStruct((8, 160, 256), BF)
    held = exchange(call(to_x_kernel, spread, (quad_me, got)), "y")
    parts = exchange(x_back_products(quad_me, held, table_ix, outer_x), QUAD)
    total = jnp.sum(parts.astype(F32), axis=0)
    pressure = to_y(total[:144]).reshape(2, 144, 128)
    low, high = total[146].reshape(2, 1, 128), total[147].reshape(2, 1, 128)
    padded = jnp.concatenate([low, pressure, high], axis=1)
    grad_x = 0.5 * (padded[:, 2:, :] - padded[:, :-2, :])
    sides = jnp.stack([total[144:146, :144], total[152:154, :144]])
    padded = jnp.concatenate([sides[:, 0, :, None], pressure, sides[:, 1, :, None]], axis=2)
    grad_y = 0.5 * (padded[:, :, 2:] - padded[:, :, :-2])
    wet_f = wet_int.astype(F32)
    shape_zero = shape_zero[:, None, None]
    shape_one = shape_one[:, None, None]
    u_correct = (-wet_f * (shape_zero * grad_x[0][None] + shape_one * grad_x[1][None])).astype(BF)
    v_correct = (-wet_f * (shape_zero * grad_y[0][None] + shape_one * grad_y[1][None])).astype(BF)
    return (u_correct, v_correct, pressure)


def solution(mesh):
    sub = Mesh(mesh.devices.reshape([n for _, n in SUB]), [name for name, _ in SUB])
    return jax.shard_map(
        body,
        mesh=sub,
        in_specs=(
            P(None, GX, GY),
            P(None, GX, GY),
            P(GX, GY),
            P(GX, GY),
            P(),
            P(),
            P(GX, None),
            P(GY, None),
            P(GX, None),
            P(GY, None),
            P(GX),
            P(GY),
            P(),
        ),
        out_specs=(P(None, GX, GY), P(None, GX, GY), P(None, GX, GY)),
        check_vma=False,
    )
```

```python
import functools

import jax
import jax.numpy as jnp
from jax import lax
from jax.experimental import pallas as pl
from jax.experimental.pallas import tpu as pltpu
from jax.sharding import Mesh
from jax.sharding import PartitionSpec as P

SUB = (("y", 8), ("xl", 2), ("c", 2), ("xh", 2), ("zh", 4), ("zl", 3))
GX = ("y", "xl", "c")
GY = ("xh", "zh", "zl")
QUAD = ("xl", "c")
BF = jnp.bfloat16
F32 = jnp.float32


def exchange(parts, axes):
    return lax.all_to_all(parts, axes, 0, 0)


def edges(block, axes, dim, count, periodic):
    forward = [(i, i + 1) for i in range(count - 1)]
    if periodic:
        forward.append((count - 1, 0))
    backward = [(target, source) for source, target in forward]
    low = lax.ppermute(lax.slice_in_dim(block, block.shape[dim] - 1, None, axis=dim), axes, forward)
    high = lax.ppermute(lax.slice_in_dim(block, 0, 1, axis=dim), axes, backward)
    return low, high


def centre_x(field):
    low, high = edges(field.astype(BF), GX, 1, 32, True)
    padded = jnp.concatenate([low.astype(F32), field, high.astype(F32)], axis=1)
    return 0.5 * (padded[:, 2:, :] - padded[:, :-2, :])


def centre_y(field):
    low, high = edges(field.astype(BF), GY, 2, 24, False)
    padded = jnp.concatenate([low.astype(F32), field, high.astype(F32)], axis=2)
    return 0.5 * (padded[:, :, 2:] - padded[:, :, :-2])


def call(kernel, out_shape, operands, scratch=(), flops=0):
    smem, vmem = pl.BlockSpec(memory_space=pltpu.SMEM), pl.BlockSpec(memory_space=pltpu.VMEM)
    outs = out_shape if isinstance(out_shape, list) else [out_shape]
    moved = sum(x.size * x.dtype.itemsize for x in list(operands[1:]) + outs)
    return pl.pallas_call(
        kernel,
        out_shape=out_shape,
        in_specs=[smem] + [vmem] * (len(operands) - 1),
        out_specs=[vmem] * len(outs) if isinstance(out_shape, list) else vmem,
        scratch_shapes=list(scratch),
        cost_estimate=pl.CostEstimate(flops=flops, bytes_accessed=moved, transcendentals=0),
        compiler_params=pltpu.CompilerParams(vmem_limit_bytes=12 << 20),
    )(*operands)


def window(place, half):
    return 9 * (place // 2) + 4 * (place % 2) + half


def quad_cut_kernel(me_ref, rows_ref, *out_refs):
    me = me_ref[0]
    for step, out_ref in enumerate(out_refs):
        other = lax.bitwise_xor(me, step)
        for y in range(8):
            start = pl.multiple_of((window(y, 0) + other) * 128, 128)
            back = lax.rem(256 - 64 * (y % 2) - 16 * other, 256)
            packed = pltpu.roll(rows_ref[:, pl.ds(start, 256)].astype(F32), back, 1)
            out_ref[:, 144 * y : 144 * (y + 1)] = packed[:, :144].astype(BF)


def quad_cut(me, rows):
    return call(quad_cut_kernel, [jax.ShapeDtypeStruct((144, 1152), BF)] * 4, (me, rows))


def quad_send(piece, step):
    return lax.ppermute(piece, QUAD, [(i, i ^ step) for i in range(4)])


def ring_cut_kernel(me_ref, first_ref, second_ref, *out_refs):
    me = me_ref[0]
    for step, out_ref in enumerate(out_refs):
        other = lax.rem(me + step, 3)
        for g in range(8):
            start = pl.multiple_of((3 * g + other) * 128, 128)
            out_ref[:128, g * 128 : (g + 1) * 128] = first_ref[:, pl.ds(start, 128)]
            out_ref[128:, g * 128 : (g + 1) * 128] = second_ref[:, pl.ds(start, 128)]


def ring_cut(me, first, second):
    return call(ring_cut_kernel, [jax.ShapeDtypeStruct((256, 1024), BF)] * 3, (me, first, second))


def ring_send(piece, step):
    return lax.ppermute(piece, "zl", [(i, (i + step) % 3) for i in range(3)])


def x_kernel(me_ref, held_ref, t0, t1, t2, t3, out_ref):
    me = me_ref[0]
    for step, table in enumerate((t0, t1, t2, t3)):
        part = jnp.dot(table[...], held_ref[...], preferred_element_type=F32)
        out_ref[lax.bitwise_xor(me, step)] = part.astype(BF)


def x_products(me, held, table):
    held = held.reshape(1152, 256)
    out = jax.ShapeDtypeStruct((4, 144, 256), BF)
    return call(x_kernel, out, (me, held, *table), flops=2 * 576 * 1152 * 256)


def y_kernel(offset, me_ref, held_ref, t0, t1, t2, out_ref, placed):
    me = me_ref[0]
    for g in range(8):
        placed[:, g * 128 : (g + 1) * 128] = held_ref[g]
    for step, table in enumerate((t0, t1, t2)):
        part = lax.dot_general(
            placed[...],
            table[offset : offset + 128, :],
            (((1,), (1,)), ((), ())),
            preferred_element_type=F32,
        )
        out_ref[lax.rem(me + 3 - step, 3)] = part.astype(BF)


def y_products(me, held, table):
    out = jax.ShapeDtypeStruct((3, 288, 128), BF)
    scratch = [pltpu.VMEM((288, 1024), BF)]
    return call(functools.partial(y_kernel, 0), out, (me, held, *table), scratch, flops=2 * 288 * 1024 * 384)


def added(got_ref):
    total = got_ref[0].astype(F32)
    for source in range(1, got_ref.shape[0]):
        total = total + got_ref[source].astype(F32)
    return total


def to_y_kernel(me_ref, got_ref, out_ref):
    total = added(got_ref).astype(BF)
    for g in range(8):
        out_ref[g, :144, :] = total[:, :128]
        out_ref[g, 144:, :] = total[:, 128:]


def scale_kernel(shift_ref, got_ref, denom_ref, out_ref):
    total = added(got_ref)
    denom = denom_ref[...]
    for mode in range(2):
        rows = slice(144 * mode, 144 * (mode + 1))
        scaled = (total[rows] / (denom + shift_ref[mode])).astype(BF)
        for g in range(8):
            out_ref[g, rows, :] = scaled


def to_x_kernel(me_ref, got_ref, out_ref):
    total = added(got_ref)
    main = total[:288].astype(BF)
    sides = jnp.concatenate(
        [
            jnp.concatenate([total[288:296], total[304:312]], axis=0),
            jnp.concatenate([total[296:304], total[312:320]], axis=0),
        ],
        axis=1,
    ).astype(BF)
    for g in range(8):
        out_ref[g, :144, :128] = main[:144]
        out_ref[g, :144, 128:] = main[144:]
        out_ref[g, 144:, :] = sides


def nt_dot(left, right):
    return lax.dot_general(left, right, (((1,), (1,)), ((), ())), preferred_element_type=F32)


def x_back_kernel(me_ref, held_ref, t0, t1, t2, t3, lo_ref, hi_ref, out_ref, placed, side, last, first, sums):
    me = me_ref[0]
    sums[...] = jnp.zeros_like(sums)
    for y in range(8):
        placed[144 * y : 144 * (y + 1), :] = held_ref[y, :144, :]
        side[:, 144 * y : 144 * (y + 1)] = held_ref[y, 144:160, :144]
    last[0] = jnp.dot(lo_ref[...], placed[...], preferred_element_type=F32)[8:16]
    first[5] = jnp.dot(hi_ref[...], placed[...], preferred_element_type=F32)[:8]
    for step, table in enumerate((t0, t1, t2, t3)):
        target = lax.bitwise_xor(me, step)
        part = jnp.dot(table[...], placed[...], preferred_element_type=F32)
        out_ref[target, :144, :] = part.astype(BF)
        last[target + 1] = part[136:144]
        first[target + 1] = part[:8]
        sums[target, :, :144] = nt_dot(side[...], table[...])
    row = lax.broadcasted_iota(jnp.int32, (16, 256), 0)
    for target in range(4):
        low = jnp.broadcast_to(last[target][7:8], (16, 256))
        high = jnp.broadcast_to(first[target + 2][:1], (16, 256))
        group = jnp.where(row == 2, low, jnp.where(row == 3, high, sums[target]))
        out_ref[target, 144:160, :] = group.astype(BF)


def x_back_products(me, held, table, outer):
    scratch = [
        pltpu.VMEM((1152, 256), BF),
        pltpu.VMEM((16, 1152), BF),
        pltpu.VMEM((5, 8, 256), F32),
        pltpu.VMEM((6, 8, 256), F32),
        pltpu.VMEM((4, 16, 256), F32),
    ]
    out = jax.ShapeDtypeStruct((4, 160, 256), BF)
    return call(x_back_kernel, out, (me, held, *table, *outer), scratch, flops=2 * 576 * 1152 * 256)


def y_back_kernel(me_ref, held_ref, t0, t1, t2, lo_ref, hi_ref, out_ref, placed, last, first):
    me = me_ref[0]
    placed[288:, :] = jnp.zeros((112, 1024), BF)
    for g in range(8):
        placed[:288, g * 128 : (g + 1) * 128] = held_ref[g]
    last[0] = lo_ref[...]
    first[4] = hi_ref[...]
    for step, table in enumerate((t0, t1, t2)):
        target = lax.rem(me + 3 - step, 3)
        out_ref[target, :288, :] = nt_dot(placed[:288, :], table[128:, :]).astype(BF)
        last[target + 1] = table[240:256, :]
        first[target + 1] = table[128:144, :]
    row = lax.broadcasted_iota(jnp.int32, (16, 128), 0)
    lane = lax.broadcasted_iota(jnp.int32, (32, 128), 1)
    for target in range(3):
        rows = jnp.concatenate([last[target], first[target + 2]], axis=0)
        for mode in range(2):
            head = nt_dot(rows, placed[144 * mode : 144 * mode + 128, :])
            rest = nt_dot(rows, placed[144 * mode + 128 : 144 * mode + 256, :])
            rest = jnp.where(lane < 16, rest, 0.0)
            group = jnp.zeros((16, 128), F32)
            for at, value in ((0, head[15:16]), (1, head[16:17]), (8, rest[15:16]), (9, rest[16:17])):
                group = jnp.where(row == at, jnp.broadcast_to(value, (16, 128)), group)
            out_ref[target, 288 + 16 * mode : 304 + 16 * mode, :] = group.astype(BF)


def y_back_products(me, held, table, outer):
    scratch = [
        pltpu.VMEM((400, 1024), BF),
        pltpu.VMEM((4, 16, 1024), BF),
        pltpu.VMEM((5, 16, 1024), BF),
    ]
    out = jax.ShapeDtypeStruct((3, 320, 128), BF)
    return call(y_back_kernel, out, (me, held, *table, *outer), scratch, flops=2 * 288 * 1024 * 384)


def ring_outer(me, table):
    low = lax.dynamic_index_in_dim(jnp.stack([t[240:256] for t in table]), (me + 1) % 3, 0, False)
    high = lax.dynamic_index_in_dim(jnp.stack([t[128:144] for t in table]), me, 0, False)
    up = [(i, i + 1) for i in range(7)]
    down = [(i + 1, i) for i in range(7)]
    return lax.ppermute(low, ("xh", "zh"), up), lax.ppermute(high, ("xh", "zh"), down)


def quad_outer(me, table):
    low = lax.dynamic_index_in_dim(jnp.stack([t[128:144] for t in table]), me ^ 3, 0, False)
    high = lax.dynamic_index_in_dim(jnp.stack([t[:16] for t in table]), me, 0, False)
    up = [(i, (i + 1) % 8) for i in range(8)]
    down = [((i + 1) % 8, i) for i in range(8)]
    return lax.ppermute(low, "y", up), lax.ppermute(high, "y", down)


def to_x(block):
    return jnp.concatenate([block[:144], block[144:]], axis=1)


def to_y(block):
    return jnp.concatenate([block[:, :128], block[:, 128:]], axis=0)


def body(
    u_flow,
    v_flow,
    sea_mask,
    bottom_level,
    mode_project,
    mode_shape,
    forward_x,
    forward_y,
    inverse_x,
    inverse_y,
    eigen_x,
    eigen_y,
    mode_shift,
):
    level_ids = lax.broadcasted_iota(jnp.int32, u_flow.shape, 0)
    wet_int = sea_mask[None] * (level_ids < bottom_level[None]).astype(jnp.int32)
    wet = wet_int.astype(BF)
    flux_u = jnp.einsum("lm,lij->mij", mode_project, u_flow * wet, preferred_element_type=F32)
    flux_v = jnp.einsum("lm,lij->mij", mode_project, v_flow * wet, preferred_element_type=F32)
    flux_u = flux_u.astype(BF).astype(F32)
    flux_v = flux_v.astype(BF).astype(F32)
    mask_f = sea_mask.astype(F32)
    divergence = (mask_f[None] * (centre_x(flux_u) + centre_y(flux_v))).astype(BF)
    quad_me = (lax.axis_index("xl") * 2 + lax.axis_index("c")).astype(jnp.int32).reshape(1)
    ring_me = lax.axis_index("zl").astype(jnp.int32).reshape(1)
    cut_fx, cut_y = quad_cut(quad_me, forward_x), ring_cut(ring_me, forward_y, inverse_y)
    divergence, y_one, fx_two = lax.optimization_barrier((divergence, ring_send(cut_y[1], 1), cut_fx[2]))
    cut_fx = [cut_fx[0], cut_fx[1], fx_two, cut_fx[3]]
    fx_two, fx_three = quad_send(cut_fx[2], 2), quad_send(cut_fx[3], 3)
    core, fx_two = lax.optimization_barrier((cut_fx[1], fx_two))
    table_fx = (cut_fx[0], quad_send(core, 1), fx_two, fx_three)
    y_two = ring_send(cut_y[2], 2)
    block = to_x(divergence.reshape(288, 128))
    held = exchange(jnp.broadcast_to(block[None], (8, 144, 256)), "y")
    held, y_two = lax.optimization_barrier((held, y_two))
    got = exchange(x_products(quad_me, held, table_fx), QUAD)
    shapes = (mode_shape[:, 0], mode_shape[:, 1])
    got, (shape_zero, shape_one) = lax.optimization_barrier((got, shapes))
    cut_ix = quad_cut(quad_me, inverse_x)
    table_y = (cut_y[0], y_one, y_two)
    spread = jax.ShapeDtypeStruct((8, 288, 128), BF)
    held = exchange(call(to_y_kernel, spread, (quad_me, got)), ("xh", "zh"))
    ix_two, ix_three = quad_send(cut_ix[2], 2), quad_send(cut_ix[3], 3)
    core, ix_two = lax.optimization_barrier((cut_ix[1], ix_two))
    table_ix = (cut_ix[0], quad_send(core, 1), ix_two, ix_three)
    denom = eigen_x[:, None] + eigen_y[None, :]
    held, table_ix, denom = lax.optimization_barrier((held, table_ix, denom))
    got = exchange(y_products(ring_me, held, table_y), "zl")
    got, table_ix, table_y = lax.optimization_barrier((got, table_ix, table_y))
    outer_y = ring_outer(ring_me[0], table_y)
    held = exchange(call(scale_kernel, spread, (mode_shift, got, denom)), ("xh", "zh"))
    outer_x = quad_outer(quad_me[0], table_ix)
    held, outer_x = lax.optimization_barrier((held, outer_x))
    got = exchange(y_back_products(ring_me, held, table_y, outer_y), "zl")
    spread = jax.ShapeDtypeStruct((8, 160, 256), BF)
    held = exchange(call(to_x_kernel, spread, (quad_me, got)), "y")
    parts = exchange(x_back_products(quad_me, held, table_ix, outer_x), QUAD)
    total = jnp.sum(parts.astype(F32), axis=0)
    pressure = to_y(total[:144]).reshape(2, 144, 128)
    low, high = total[146].reshape(2, 1, 128), total[147].reshape(2, 1, 128)
    padded = jnp.concatenate([low, pressure, high], axis=1)
    grad_x = 0.5 * (padded[:, 2:, :] - padded[:, :-2, :])
    sides = jnp.stack([total[144:146, :144], total[152:154, :144]])
    padded = jnp.concatenate([sides[:, 0, :, None], pressure, sides[:, 1, :, None]], axis=2)
    grad_y = 0.5 * (padded[:, :, 2:] - padded[:, :, :-2])
    wet_f = wet_int.astype(F32)
    shape_zero = shape_zero[:, None, None]
    shape_one = shape_one[:, None, None]
    u_correct = (-wet_f * (shape_zero * grad_x[0][None] + shape_one * grad_x[1][None])).astype(BF)
    v_correct = (-wet_f * (shape_zero * grad_y[0][None] + shape_one * grad_y[1][None])).astype(BF)
    return (u_correct, v_correct, pressure)


def solution(mesh):
    sub = Mesh(mesh.devices.reshape([n for _, n in SUB]), [name for name, _ in SUB])
    return jax.shard_map(
        body,
        mesh=sub,
        in_specs=(
            P(None, GX, GY),
            P(None, GX, GY),
            P(GX, GY),
            P(GX, GY),
            P(),
            P(),
            P(GX, None),
            P(GY, None),
            P(GX, None),
            P(GY, None),
            P(GX),
            P(GY),
            P(),
        ),
        out_specs=(P(None, GX, GY), P(None, GX, GY), P(None, GX, GY)),
        check_vma=False,
    )
```

```python
import functools

import jax
import jax.numpy as jnp
from jax import lax
from jax.experimental import pallas as pl
from jax.experimental.pallas import tpu as pltpu
from jax.sharding import Mesh
from jax.sharding import PartitionSpec as P

SUB = (("y", 8), ("xl", 2), ("c", 2), ("xh", 2), ("zh", 4), ("zl", 3))
GX = ("y", "xl", "c")
GY = ("xh", "zh", "zl")
QUAD = ("xl", "c")
BF = jnp.bfloat16
F32 = jnp.float32


def exchange(parts, axes):
    return lax.all_to_all(parts, axes, 0, 0)


def edges(block, axes, dim, count, periodic):
    forward = [(i, i + 1) for i in range(count - 1)]
    if periodic:
        forward.append((count - 1, 0))
    backward = [(target, source) for source, target in forward]
    low = lax.ppermute(lax.slice_in_dim(block, block.shape[dim] - 1, None, axis=dim), axes, forward)
    high = lax.ppermute(lax.slice_in_dim(block, 0, 1, axis=dim), axes, backward)
    return low, high


def centre_x(field):
    low, high = edges(field.astype(BF), GX, 1, 32, True)
    padded = jnp.concatenate([low.astype(F32), field, high.astype(F32)], axis=1)
    return 0.5 * (padded[:, 2:, :] - padded[:, :-2, :])


def centre_y(field):
    low, high = edges(field.astype(BF), GY, 2, 24, False)
    padded = jnp.concatenate([low.astype(F32), field, high.astype(F32)], axis=2)
    return 0.5 * (padded[:, :, 2:] - padded[:, :, :-2])


def call(kernel, out_shape, operands, scratch=(), flops=0):
    smem, vmem = pl.BlockSpec(memory_space=pltpu.SMEM), pl.BlockSpec(memory_space=pltpu.VMEM)
    outs = out_shape if isinstance(out_shape, list) else [out_shape]
    moved = sum(x.size * x.dtype.itemsize for x in list(operands[1:]) + outs)
    return pl.pallas_call(
        kernel,
        out_shape=out_shape,
        in_specs=[smem] + [vmem] * (len(operands) - 1),
        out_specs=[vmem] * len(outs) if isinstance(out_shape, list) else vmem,
        scratch_shapes=list(scratch),
        cost_estimate=pl.CostEstimate(flops=flops, bytes_accessed=moved, transcendentals=0),
        compiler_params=pltpu.CompilerParams(vmem_limit_bytes=12 << 20),
    )(*operands)


def window(place, half):
    return 9 * (place // 2) + 4 * (place % 2) + half


def quad_cut_kernel(me_ref, rows_ref, *out_refs):
    me = me_ref[0]
    for step, out_ref in enumerate(out_refs):
        other = lax.bitwise_xor(me, step)
        for y in range(8):
            start = pl.multiple_of((window(y, 0) + other) * 128, 128)
            back = lax.rem(256 - 64 * (y % 2) - 16 * other, 256)
            packed = pltpu.roll(rows_ref[:, pl.ds(start, 256)].astype(F32), back, 1)
            out_ref[:, 144 * y : 144 * (y + 1)] = packed[:, :144].astype(BF)


def quad_cut(me, rows):
    return call(quad_cut_kernel, [jax.ShapeDtypeStruct((144, 1152), BF)] * 4, (me, rows))


def quad_send(piece, step):
    return lax.ppermute(piece, QUAD, [(i, i ^ step) for i in range(4)])


def ring_cut_kernel(me_ref, first_ref, second_ref, *out_refs):
    me = me_ref[0]
    for step, out_ref in enumerate(out_refs):
        other = lax.rem(me + step, 3)
        for g in range(8):
            start = pl.multiple_of((3 * g + other) * 128, 128)
            out_ref[:128, g * 128 : (g + 1) * 128] = first_ref[:, pl.ds(start, 128)]
            out_ref[128:, g * 128 : (g + 1) * 128] = second_ref[:, pl.ds(start, 128)]


def ring_cut(me, first, second):
    return call(ring_cut_kernel, [jax.ShapeDtypeStruct((256, 1024), BF)] * 3, (me, first, second))


def ring_send(piece, step):
    return lax.ppermute(piece, "zl", [(i, (i + step) % 3) for i in range(3)])


def x_kernel(me_ref, held_ref, t0, t1, t2, t3, out_ref):
    me = me_ref[0]
    for step, table in enumerate((t0, t1, t2, t3)):
        part = jnp.dot(table[...], held_ref[...], preferred_element_type=F32)
        out_ref[lax.bitwise_xor(me, step)] = part.astype(BF)


def x_products(me, held, table):
    held = held.reshape(1152, 256)
    out = jax.ShapeDtypeStruct((4, 144, 256), BF)
    return call(x_kernel, out, (me, held, *table), flops=2 * 576 * 1152 * 256)


def y_kernel(offset, me_ref, held_ref, t0, t1, t2, out_ref, placed):
    me = me_ref[0]
    for g in range(8):
        placed[:, g * 128 : (g + 1) * 128] = held_ref[g]
    for step, table in enumerate((t0, t1, t2)):
        part = lax.dot_general(
            placed[...],
            table[offset : offset + 128, :],
            (((1,), (1,)), ((), ())),
            preferred_element_type=F32,
        )
        out_ref[lax.rem(me + 3 - step, 3)] = part.astype(BF)


def y_products(me, held, table):
    out = jax.ShapeDtypeStruct((3, 288, 128), BF)
    scratch = [pltpu.VMEM((288, 1024), BF)]
    return call(functools.partial(y_kernel, 0), out, (me, held, *table), scratch, flops=2 * 288 * 1024 * 384)


def added(got_ref):
    total = got_ref[0].astype(F32)
    for source in range(1, got_ref.shape[0]):
        total = total + got_ref[source].astype(F32)
    return total


def spread_kernel(me_ref, block_ref, out_ref):
    for y in range(8):
        out_ref[y, :, :128] = block_ref[0]
        out_ref[y, :, 128:] = block_ref[1]


def to_y_kernel(me_ref, got_ref, out_ref):
    total = added(got_ref).astype(BF)
    for g in range(8):
        out_ref[g, :144, :] = total[:, :128]
        out_ref[g, 144:, :] = total[:, 128:]


def scale_kernel(shift_ref, got_ref, denom_ref, out_ref):
    total = added(got_ref)
    denom = denom_ref[...]
    for mode in range(2):
        rows = slice(144 * mode, 144 * (mode + 1))
        scaled = (total[rows] / (denom + shift_ref[mode])).astype(BF)
        for g in range(8):
            out_ref[g, rows, :] = scaled


def to_x_kernel(me_ref, got_ref, out_ref):
    total = added(got_ref)
    main = total[:288].astype(BF)
    sides = jnp.concatenate(
        [
            jnp.concatenate([total[288:296], total[304:312]], axis=0),
            jnp.concatenate([total[296:304], total[312:320]], axis=0),
        ],
        axis=1,
    ).astype(BF)
    for g in range(8):
        out_ref[g, :144, :128] = main[:144]
        out_ref[g, :144, 128:] = main[144:]
        out_ref[g, 144:, :] = sides


def nt_dot(left, right):
    return lax.dot_general(left, right, (((1,), (1,)), ((), ())), preferred_element_type=F32)


def x_back_kernel(me_ref, held_ref, t0, t1, t2, t3, lo_ref, hi_ref, out_ref, placed, side, last, first, sums):
    me = me_ref[0]
    sums[...] = jnp.zeros_like(sums)
    for y in range(8):
        placed[144 * y : 144 * (y + 1), :] = held_ref[y, :144, :]
        side[:, 144 * y : 144 * (y + 1)] = held_ref[y, 144:160, :144]
    last[0] = jnp.dot(lo_ref[...], placed[...], preferred_element_type=F32)[8:16]
    first[5] = jnp.dot(hi_ref[...], placed[...], preferred_element_type=F32)[:8]
    for step, table in enumerate((t0, t1, t2, t3)):
        target = lax.bitwise_xor(me, step)
        part = jnp.dot(table[...], placed[...], preferred_element_type=F32)
        out_ref[target, :144, :] = part.astype(BF)
        last[target + 1] = part[136:144]
        first[target + 1] = part[:8]
        sums[target, :, :144] = nt_dot(side[...], table[...])
    row = lax.broadcasted_iota(jnp.int32, (16, 256), 0)
    for target in range(4):
        low = jnp.broadcast_to(last[target][7:8], (16, 256))
        high = jnp.broadcast_to(first[target + 2][:1], (16, 256))
        group = jnp.where(row == 2, low, jnp.where(row == 3, high, sums[target]))
        out_ref[target, 144:160, :] = group.astype(BF)


def x_back_products(me, held, table, outer):
    scratch = [
        pltpu.VMEM((1152, 256), BF),
        pltpu.VMEM((16, 1152), BF),
        pltpu.VMEM((5, 8, 256), F32),
        pltpu.VMEM((6, 8, 256), F32),
        pltpu.VMEM((4, 16, 256), F32),
    ]
    out = jax.ShapeDtypeStruct((4, 160, 256), BF)
    return call(x_back_kernel, out, (me, held, *table, *outer), scratch, flops=2 * 576 * 1152 * 256)


def y_back_kernel(me_ref, held_ref, t0, t1, t2, lo_ref, hi_ref, out_ref, placed, last, first):
    me = me_ref[0]
    placed[288:, :] = jnp.zeros((112, 1024), BF)
    for g in range(8):
        placed[:288, g * 128 : (g + 1) * 128] = held_ref[g]
    last[0] = lo_ref[...]
    first[4] = hi_ref[...]
    for step, table in enumerate((t0, t1, t2)):
        target = lax.rem(me + 3 - step, 3)
        out_ref[target, :288, :] = nt_dot(placed[:288, :], table[128:, :]).astype(BF)
        last[target + 1] = table[240:256, :]
        first[target + 1] = table[128:144, :]
    row = lax.broadcasted_iota(jnp.int32, (16, 128), 0)
    lane = lax.broadcasted_iota(jnp.int32, (32, 128), 1)
    for target in range(3):
        rows = jnp.concatenate([last[target], first[target + 2]], axis=0)
        for mode in range(2):
            head = nt_dot(rows, placed[144 * mode : 144 * mode + 128, :])
            rest = nt_dot(rows, placed[144 * mode + 128 : 144 * mode + 256, :])
            rest = jnp.where(lane < 16, rest, 0.0)
            group = jnp.zeros((16, 128), F32)
            for at, value in ((0, head[15:16]), (1, head[16:17]), (8, rest[15:16]), (9, rest[16:17])):
                group = jnp.where(row == at, jnp.broadcast_to(value, (16, 128)), group)
            out_ref[target, 288 + 16 * mode : 304 + 16 * mode, :] = group.astype(BF)


def y_back_products(me, held, table, outer):
    scratch = [
        pltpu.VMEM((400, 1024), BF),
        pltpu.VMEM((4, 16, 1024), BF),
        pltpu.VMEM((5, 16, 1024), BF),
    ]
    out = jax.ShapeDtypeStruct((3, 320, 128), BF)
    return call(y_back_kernel, out, (me, held, *table, *outer), scratch, flops=2 * 288 * 1024 * 384)


def ring_outer(me, table):
    low = lax.dynamic_index_in_dim(jnp.stack([t[240:256] for t in table]), (me + 1) % 3, 0, False)
    high = lax.dynamic_index_in_dim(jnp.stack([t[128:144] for t in table]), me, 0, False)
    up = [(i, i + 1) for i in range(7)]
    down = [(i + 1, i) for i in range(7)]
    return lax.ppermute(low, ("xh", "zh"), up), lax.ppermute(high, ("xh", "zh"), down)


def quad_outer(me, table):
    low = lax.dynamic_index_in_dim(jnp.stack([t[128:144] for t in table]), me ^ 3, 0, False)
    high = lax.dynamic_index_in_dim(jnp.stack([t[:16] for t in table]), me, 0, False)
    up = [(i, (i + 1) % 8) for i in range(8)]
    down = [((i + 1) % 8, i) for i in range(8)]
    return lax.ppermute(low, "y", up), lax.ppermute(high, "y", down)


def to_y(block):
    return jnp.concatenate([block[:, :128], block[:, 128:]], axis=0)


def body(
    u_flow,
    v_flow,
    sea_mask,
    bottom_level,
    mode_project,
    mode_shape,
    forward_x,
    forward_y,
    inverse_x,
    inverse_y,
    eigen_x,
    eigen_y,
    mode_shift,
):
    level_ids = lax.broadcasted_iota(jnp.int32, u_flow.shape, 0)
    wet_int = sea_mask[None] * (level_ids < bottom_level[None]).astype(jnp.int32)
    wet = wet_int.astype(BF)
    flux_u = jnp.einsum("lm,lij->mij", mode_project, u_flow * wet, preferred_element_type=F32)
    flux_v = jnp.einsum("lm,lij->mij", mode_project, v_flow * wet, preferred_element_type=F32)
    flux_u = flux_u.astype(BF).astype(F32)
    flux_v = flux_v.astype(BF).astype(F32)
    mask_f = sea_mask.astype(F32)
    divergence = (mask_f[None] * (centre_x(flux_u) + centre_y(flux_v))).astype(BF)
    quad_me = (lax.axis_index("xl") * 2 + lax.axis_index("c")).astype(jnp.int32).reshape(1)
    ring_me = lax.axis_index("zl").astype(jnp.int32).reshape(1)
    cut_fx, cut_y = quad_cut(quad_me, forward_x), ring_cut(ring_me, forward_y, inverse_y)
    divergence, y_one, fx_two = lax.optimization_barrier((divergence, ring_send(cut_y[1], 1), cut_fx[2]))
    cut_fx = [cut_fx[0], cut_fx[1], fx_two, cut_fx[3]]
    fx_two, fx_three = quad_send(cut_fx[2], 2), quad_send(cut_fx[3], 3)
    core, fx_two = lax.optimization_barrier((cut_fx[1], fx_two))
    table_fx = (cut_fx[0], quad_send(core, 1), fx_two, fx_three)
    y_two = ring_send(cut_y[2], 2)
    spread = jax.ShapeDtypeStruct((8, 144, 256), BF)
    held = exchange(call(spread_kernel, spread, (quad_me, divergence)), "y")
    held, y_two = lax.optimization_barrier((held, y_two))
    got = exchange(x_products(quad_me, held, table_fx), QUAD)
    shapes = (mode_shape[:, 0], mode_shape[:, 1])
    got, (shape_zero, shape_one) = lax.optimization_barrier((got, shapes))
    cut_ix = quad_cut(quad_me, inverse_x)
    table_y = (cut_y[0], y_one, y_two)
    spread = jax.ShapeDtypeStruct((8, 288, 128), BF)
    held = exchange(call(to_y_kernel, spread, (quad_me, got)), ("xh", "zh"))
    ix_two, ix_three = quad_send(cut_ix[2], 2), quad_send(cut_ix[3], 3)
    core, ix_two = lax.optimization_barrier((cut_ix[1], ix_two))
    table_ix = (cut_ix[0], quad_send(core, 1), ix_two, ix_three)
    denom = eigen_x[:, None] + eigen_y[None, :]
    held, table_ix, denom = lax.optimization_barrier((held, table_ix, denom))
    got = exchange(y_products(ring_me, held, table_y), "zl")
    got, table_ix, table_y = lax.optimization_barrier((got, table_ix, table_y))
    outer_y = ring_outer(ring_me[0], table_y)
    held = exchange(call(scale_kernel, spread, (mode_shift, got, denom)), ("xh", "zh"))
    outer_x = quad_outer(quad_me[0], table_ix)
    held, outer_x = lax.optimization_barrier((held, outer_x))
    got = exchange(y_back_products(ring_me, held, table_y, outer_y), "zl")
    spread = jax.ShapeDtypeStruct((8, 160, 256), BF)
    held = exchange(call(to_x_kernel, spread, (quad_me, got)), "y")
    parts = exchange(x_back_products(quad_me, held, table_ix, outer_x), QUAD)
    total = jnp.sum(parts.astype(F32), axis=0)
    pressure = to_y(total[:144]).reshape(2, 144, 128)
    low, high = total[146].reshape(2, 1, 128), total[147].reshape(2, 1, 128)
    padded = jnp.concatenate([low, pressure, high], axis=1)
    grad_x = 0.5 * (padded[:, 2:, :] - padded[:, :-2, :])
    sides = jnp.stack([total[144:146, :144], total[152:154, :144]])
    padded = jnp.concatenate([sides[:, 0, :, None], pressure, sides[:, 1, :, None]], axis=2)
    grad_y = 0.5 * (padded[:, :, 2:] - padded[:, :, :-2])
    wet_f = wet_int.astype(F32)
    shape_zero = shape_zero[:, None, None]
    shape_one = shape_one[:, None, None]
    u_correct = (-wet_f * (shape_zero * grad_x[0][None] + shape_one * grad_x[1][None])).astype(BF)
    v_correct = (-wet_f * (shape_zero * grad_y[0][None] + shape_one * grad_y[1][None])).astype(BF)
    return (u_correct, v_correct, pressure)


def solution(mesh):
    sub = Mesh(mesh.devices.reshape([n for _, n in SUB]), [name for name, _ in SUB])
    return jax.shard_map(
        body,
        mesh=sub,
        in_specs=(
            P(None, GX, GY),
            P(None, GX, GY),
            P(GX, GY),
            P(GX, GY),
            P(),
            P(),
            P(GX, None),
            P(GY, None),
            P(GX, None),
            P(GY, None),
            P(GX),
            P(GY),
            P(),
        ),
        out_specs=(P(None, GX, GY), P(None, GX, GY), P(None, GX, GY)),
        check_vma=False,
    )
```
